128 devices in a mesh: row: 16 (over y, z), col: 8 (over x, core).
Axes of the slice: x: 4, y: 4, z: 4, core: 2. Of those that a mesh axis runs over, the one named last changes fastest.
Arguments:
- x_points: float32 [64, 262144], P(None, ('row', 'col')), as said below
- y_points: float32 [64, 262144], P(None, ('row', 'col')), as said below
- x_logmass: float32 [262144], P(('row', 'col')), may hold values from -1 to 1
- y_logmass: float32 [262144], P(('row', 'col')), may hold values from -1 to 1
- x_sizes: int32 [128, 8], P(('row', 'col')), may hold values from 1 to 256, 1664 in all within a row
- y_sizes: int32 [128, 8], P(('row', 'col')), may hold values from 1 to 256, 1664 in all within a row
- cross_pairs: int32 [1024, 7], P(('row', 'col')), may hold values from 0 to 1023, as said below
- xself_pairs: int32 [1024, 2], P(('row', 'col')), may hold values from 0 to 1023, as said below
- yself_pairs: int32 [1024, 2], P(('row', 'col')), may hold values from 0 to 1023, as said below
Outputs:
- x_cross: float32 [262144], P(('row', 'col'))
- y_cross: float32 [262144], P(('row', 'col'))
- x_self: float32 [262144], P(('row', 'col'))
- y_self: float32 [262144], P(('row', 'col'))
The draws below stay inside these ranges and needn't reach their ends.
Inputs may be any that keep to these rules, and one draw needn't show every extreme that they name: Each row of a device's lists names different clusters, none held by the device itself. Counting the entries of cross_pairs, xself_pairs and yself_pairs in the rows of one device's 8 clusters, a device is named either never or exactly 1 times; the named clusters of one device in these entries are all different. A self partner lies on the device 1 to 63 places after the lister's device, cyclically, so no unordered pair is listed twice. `xself_pairs`: as stated for cross_pairs. `yself_pairs`: as stated for cross_pairs. `x_sizes`: each row sums to 1664. `y_sizes`: each row sums to 1664. `x_points`: points of a cluster scatter around a common centre. `y_points`: points of a cluster scatter around a common centre.
All inputs are finite; a program needn't handle non-finite values.
Results may differ from the reference program's by a relative error of at most 0.0003.
Values sent between devices are 32-bit elements; how exact they have to be, the bound alone decides.
No kernel may reach another device: no remote copies, remote signals or barrier semaphores. Data moves between devices by JAX's collectives and lax.ppermute only.
A program may use at most 128 MiB of HBM per device.

```python
import math
import jax
import jax.numpy as jnp
import numpy as np
from jax import lax

D = 64
CS = 256
CL = 8
K = 8
KS = 2
ITERS = 3
NDEV = 128
NCL = 1024
NPTS = 262144
CAP = 1
PTS_DEV = 1664


def pair_tables(key):
    self_slots = 2 * CL * KS
    cross_slots = CL * (K - 1)
    self_owned = self_slots // CAP
    cross_owned = cross_slots // CAP

    def one_device(device):
        device_key = jax.random.fold_in(key, device)
        key_list = jax.random.split(device_key, 5)
        deltas = jax.random.permutation(key_list[0], NDEV // 2 - 1)[:self_owned] + 1
        self_owner = (device + deltas) % NDEV
        rank_order = jax.random.permutation(key_list[1], NDEV)
        taken = jnp.zeros((NDEV,), jnp.int32).at[self_owner].set(1).at[device].set(1)
        owner_score = rank_order + NDEV * taken
        cross_owner = jnp.argsort(owner_score, stable=True)[:cross_owned].astype(jnp.int32)
        owner_list = jnp.concatenate([self_owner, cross_owner])
        pick_keys = jax.random.split(key_list[2], self_owned + cross_owned)
        partner_pick = jax.vmap(lambda pick_key: jax.random.permutation(pick_key, CL)[:CAP])(pick_keys)
        partner = owner_list[:, None] * CL + partner_pick
        self_flat = partner[:self_owned].reshape(-1)
        cross_flat = partner[self_owned:].reshape(-1)
        self_perm = jax.random.permutation(key_list[3], self_slots)
        cross_perm = jax.random.permutation(key_list[4], cross_slots)
        self_ids = jnp.zeros((self_slots,), jnp.int32).at[self_perm].set(self_flat)
        cross_ids = jnp.zeros((cross_slots,), jnp.int32).at[cross_perm].set(cross_flat)
        return (cross_ids.reshape(CL, K - 1), self_ids[:CL * KS].reshape(CL, KS), self_ids[CL * KS:].reshape(CL, KS))
    cross_table, xself_table, yself_table = jax.vmap(one_device)(jnp.arange(NDEV, dtype=jnp.int32))
    return (cross_table.reshape(NCL, K - 1), xself_table.reshape(NCL, KS), yself_table.reshape(NCL, KS))


def draw_cross_pairs(key, part):
    return pair_tables(jax.random.fold_in(key, 11))[0]


def draw_xself_pairs(key, part):
    return pair_tables(jax.random.fold_in(key, 11))[1]


def draw_yself_pairs(key, part):
    return pair_tables(jax.random.fold_in(key, 11))[2]


def cluster_centers(key):
    return 0.05 * jax.random.normal(jax.random.fold_in(key, 23), (D, NCL, 1), jnp.float32)


def cluster_noise(key, salt):
    unit = jax.random.normal(jax.random.fold_in(key, salt), (D, NCL, CS), jnp.float32)
    return 0.1 * unit


def draw_x_points(key, part):
    centers = cluster_centers(key)
    return (centers + cluster_noise(key, 31)).reshape(D, NPTS)


def draw_y_points(key, part):
    centers = cluster_centers(key)
    direction = jax.random.normal(jax.random.fold_in(key, 37), (D, NCL, 1), jnp.float32)
    offset = 0.1 * direction
    return (centers + offset + cluster_noise(key, 41)).reshape(D, NPTS)


def block_scale(own_key, extent, cuts, low, top_value):
    loudness = 1.0
    for dim, parts in cuts:
        steps = jax.random.uniform(jax.random.fold_in(jax.random.fold_in(own_key, 6), dim), (parts,), jnp.float32, low / len(cuts), top_value / len(cuts))
        loudness = loudness * jnp.repeat(jnp.exp(steps), extent[dim] // parts).reshape((-1,) + (1,) * (len(extent) - 1 - dim))
    return loudness


def split_up(count, total, bound, slope):
    loads = [(1 << 20) // math.isqrt(rank ** slope) + 1 for rank in range(2, count + 1)]
    surplus, given = total - bound - (count - 1), [1] * (count - 1)
    while surplus > 0:
        free = [i for i in range(count - 1) if given[i] < bound]
        mass, budget = sum([loads[i] for i in free]), surplus
        for i in free:
            extra = min(bound - given[i], max(1, budget * loads[i] // mass), surplus)
            given[i] = given[i] + extra
            surplus = surplus - extra
    return np.array([bound] + given)


def ragged(rng, count, total, bound, lean):
    if count == 2:
        one = jax.random.randint(rng, (), max(1, total - bound), min(bound, total - 1) + 1)
        return jnp.stack([one, total - one])
    tallies = jnp.asarray(split_up(count, total, bound, lean), jnp.int32)
    pairs = (count - 1) // 2
    source_of, taker = tallies[1:1 + 2 * pairs:2], tallies[2:2 + 2 * pairs:2]
    margin = jnp.minimum(source_of - 1, bound - taker)
    shifted = jax.random.randint(jax.random.fold_in(rng, 1), (pairs,), 0, 1 << 20) % (margin + 1)
    tallies = tallies.at[1:1 + 2 * pairs:2].set(source_of - shifted).at[2:2 + 2 * pairs:2].set(taker + shifted)
    return tallies[jax.random.permutation(jax.random.fold_in(rng, 2), count)]


def setup_inputs(seed: int = 0) -> dict:
    seeds = jax.random.split(jax.random.key(seed), 10)
    x_points = draw_x_points(jax.random.fold_in(seeds[9], 71), 0)
    y_points = draw_y_points(jax.random.fold_in(seeds[9], 71), 0)
    x_logmass = jnp.clip(jax.random.uniform(seeds[2], (NPTS,), jnp.float32, -1.0, 1.0) * block_scale(seeds[2], (NPTS,), ((0, 128),), -0.4, 0.0), -1.0, 1.0)
    y_logmass = jnp.clip(jax.random.uniform(seeds[3], (NPTS,), jnp.float32, -1.0, 1.0) * block_scale(seeds[3], (NPTS,), ((0, 128),), -0.4, 0.0), -1.0, 1.0)
    x_sizes = jax.vmap(lambda own: ragged(own, CL, PTS_DEV, CS, 1))(jax.random.split(seeds[4], NDEV)).reshape((NDEV, CL)).astype(jnp.int32)
    y_sizes = jax.vmap(lambda own: ragged(own, CL, PTS_DEV, CS, 1))(jax.random.split(seeds[5], NDEV)).reshape((NDEV, CL)).astype(jnp.int32)
    cross_pairs = draw_cross_pairs(jax.random.fold_in(seeds[9], 71), 0)
    xself_pairs = draw_xself_pairs(jax.random.fold_in(seeds[9], 71), 0)
    yself_pairs = draw_yself_pairs(jax.random.fold_in(seeds[9], 71), 0)
    return {"x_points": x_points, "y_points": y_points, "x_logmass": x_logmass, "y_logmass": y_logmass, "x_sizes": x_sizes, "y_sizes": y_sizes, "cross_pairs": cross_pairs, "xself_pairs": xself_pairs, "yself_pairs": yself_pairs}


EPSILON = 0.5
DAMPING = 2.0 / (2.0 + 0.5)
NEGATIVE = -1.0e30
HIGHEST = lax.Precision.HIGHEST


def tile_terms(row_coords, row_half, row_offset, col_coords, col_half, col_offset):
    inner = jnp.einsum("ndi,ndj->nij", row_coords, col_coords, precision=HIGHEST)
    scaled = (row_half[:, :, None] + col_half[:, None, :] - inner) / EPSILON
    row_score = col_offset[:, None, :] - scaled
    row_peak = jnp.max(row_score, axis=2)
    row_total = jnp.sum(jnp.exp(row_score - row_peak[:, :, None]), axis=2)
    col_score = row_offset[:, :, None] - scaled
    col_peak = jnp.max(col_score, axis=1)
    col_total = jnp.sum(jnp.exp(col_score - col_peak[:, None, :]), axis=1)
    return row_peak, row_total, col_peak, col_total


def reference(x_points, y_points, x_logmass, y_logmass, x_sizes, y_sizes, cross_pairs, xself_pairs, yself_pairs):
    cluster_total = x_sizes.size
    feature_dim = x_points.shape[0]
    members = x_points.shape[1] // cluster_total
    stacked = jnp.concatenate([x_points.reshape(feature_dim, cluster_total, members), y_points.reshape(feature_dim, cluster_total, members)], axis=1).transpose(1, 0, 2)
    halves = 0.5 * jnp.sum(stacked * stacked, axis=1)
    counts = jnp.concatenate([x_sizes.reshape(-1), y_sizes.reshape(-1)])
    position = jnp.arange(members, dtype=jnp.int32)
    valid_mask = position[None, :] < counts[:, None]
    masses = jnp.where(valid_mask, jnp.concatenate([x_logmass, y_logmass]).reshape(2 * cluster_total, members), NEGATIVE)
    own_cluster = jnp.arange(cluster_total, dtype=jnp.int32)
    cross_count = cross_pairs.shape[1]
    self_count = xself_pairs.shape[1]
    cross_rows = jnp.repeat(own_cluster, cross_count)
    self_rows = jnp.repeat(own_cluster, self_count)
    cross_cols = (cluster_total + cross_pairs.reshape(-1)).astype(jnp.int32)
    x_partner = xself_pairs.reshape(-1).astype(jnp.int32)
    y_partner = yself_pairs.reshape(-1).astype(jnp.int32)
    base = cluster_total
    row_index = jnp.concatenate([own_cluster, cross_rows, self_rows, base + self_rows, own_cluster, base + own_cluster])
    row_potential = jnp.concatenate([own_cluster, cross_rows, 2 * base + self_rows, 3 * base + self_rows, 2 * base + own_cluster, 3 * base + own_cluster])
    col_index = jnp.concatenate([base + own_cluster, cross_cols, x_partner, base + y_partner, own_cluster, base + own_cluster])
    col_potential = jnp.concatenate([base + own_cluster, cross_cols, 2 * base + x_partner, 3 * base + y_partner, 2 * base + own_cluster, 3 * base + own_cluster])
    col_target = jnp.concatenate([base + own_cluster, cross_cols, 2 * base + x_partner, 3 * base + y_partner, jnp.full((2 * base,), 4 * base, jnp.int32)])
    targets = jnp.concatenate([row_potential, col_target])
    tile_batch = 64
    potentials = jnp.zeros((4 * base, members), jnp.float32)
    for iteration in range(ITERS):
        row_offset = masses[row_index] + potentials[row_potential] / EPSILON
        col_offset = masses[col_index] + potentials[col_potential] / EPSILON

        def sweep_tiles(indices):
            rows_at, cols_at, row_part, col_part = indices
            return tile_terms(stacked[rows_at], halves[rows_at], row_part, stacked[cols_at], halves[cols_at], col_part)

        tile_out = lax.map(sweep_tiles, (row_index.reshape(-1, tile_batch), col_index.reshape(-1, tile_batch), row_offset.reshape(-1, tile_batch, members), col_offset.reshape(-1, tile_batch, members)))
        row_peak, row_total, col_peak, col_total = [part.reshape(-1, members) for part in tile_out]
        peak_all = jnp.concatenate([row_peak, col_peak])
        totals = jnp.concatenate([row_total, col_total])
        segment_top = jax.ops.segment_max(peak_all, targets, num_segments=4 * base + 1)
        summed = jax.ops.segment_sum(totals * jnp.exp(peak_all - segment_top[targets]), targets, num_segments=4 * base + 1)
        log_total = segment_top[:4 * base] + jnp.log(summed[:4 * base])
        potentials = 0.5 * (potentials - DAMPING * EPSILON * log_total)
    finals = jnp.where(jnp.concatenate([valid_mask, valid_mask]), potentials, 0.0)
    return (finals[:base].reshape(-1), finals[base:2 * base].reshape(-1), finals[2 * base:3 * base].reshape(-1), finals[3 * base:].reshape(-1))
```

```python
import functools

import jax
import jax.numpy as jnp
from jax import lax
from jax.experimental import pallas as pl
from jax.experimental.pallas import tpu as pltpu
from jax.sharding import PartitionSpec as P

ITERS = 3
EPSILON = 0.5
DAMPING = 2.0 / (2.0 + 0.5)
NEGATIVE = -1e30
REAL = -1e29
LOG2E = 1.4426950408889634
LN2 = 0.6931471805599453
TINY = 2.0**-90
HUGE = 2.0**90
AXES = ("row", "col")

D = 64
CS = 256
CL = 8
HALF = 128
ROWS = 2 * D + 8
GROUP = 2
BF16 = jnp.bfloat16
F32 = jnp.float32


def lists(cross, xself, yself):
    for table, kind in ((cross, 0), (xself, 1), (yself, 2)):
        for c in range(table.shape[0]):
            for k in range(table.shape[1]):
                yield kind, c, k, table[c, k]


def bias_of(weight, half, potential):
    return LOG2E * (weight + (potential - half) / EPSILON)


def push_kernel(
    cross, xself, yself, x_sizes, y_sizes, x_ref, y_ref, x_mass, y_mass,
    send, weight_ref, half_ref, bias_ref, aux, sems,
):
    devices = send.shape[0]
    requests = list(lists(cross, xself, yself))
    for kind, c, _, named in requests:
        owner = named // CL
        source = y_ref if kind == 2 else x_ref
        for h in range(2):
            pltpu.make_async_copy(
                source.at[:, pl.ds(c * CS + h * HALF, HALF)],
                send.at[owner, pl.ds(h * D, D), :],
                sems.at[0],
            ).start()
    row = lax.broadcasted_iota(jnp.int32, (2 * CL, HALF), 0)
    position = (row % 2) * HALF + lax.broadcasted_iota(jnp.int32, (2 * CL, HALF), 1)
    for side, (points, sizes, mass) in enumerate(
        ((x_ref, x_sizes, x_mass), (y_ref, y_sizes, y_mass))
    ):
        count = jnp.zeros((2 * CL, HALF), jnp.int32)
        for c in range(CL):
            count = jnp.where(row // 2 == c, sizes[0, c], count)
        base = side * 2 * CL
        weight_ref[base : base + 2 * CL, :] = jnp.where(position < count, mass[...], NEGATIVE)
        for t in range(2 * CL):
            piece = points[:, t * HALF : (t + 1) * HALF]
            half_ref[base + t : base + t + 1, :] = 0.5 * jnp.sum(piece * piece, axis=0, keepdims=True)
    bias = bias_of(weight_ref[...], half_ref[...], 0.0)
    bias_ref[0 : 4 * CL, :] = bias
    bias_ref[4 * CL : 8 * CL, :] = bias
    aux[...] = jnp.zeros_like(aux)
    for kind, c, _, named in requests:
        owner = named // CL
        base = (2 * CL if kind == 2 else 0) + 2 * c
        aux[owner, 0:2, :] = bias_ref[base : base + 2, :]
        code = (kind * CL + named % CL + 1).astype(F32)
        aux[owner, 2:3, :] = jnp.full((1, HALF), code, F32)
    tail = pltpu.make_async_copy(aux, send.at[:, pl.ds(2 * D, 8), :], sems.at[1])
    tail.start()
    tail.wait()
    sent = send.at[pl.ds(0, len(requests)), pl.ds(0, 2 * D), :]
    pltpu.make_async_copy(sent, sent, sems.at[0]).wait()


def push(cross, xself, yself, x_sizes, y_sizes, x, y, x_mass, y_mass, devices):
    smem = pl.BlockSpec(memory_space=pltpu.SMEM)
    vmem = pl.BlockSpec(memory_space=pltpu.VMEM)
    return pl.pallas_call(
        push_kernel,
        out_shape=(
            jax.ShapeDtypeStruct((devices, ROWS, HALF), F32),
            jax.ShapeDtypeStruct((4 * CL, HALF), F32),
            jax.ShapeDtypeStruct((4 * CL, HALF), F32),
            jax.ShapeDtypeStruct((8 * CL, HALF), F32),
        ),
        in_specs=[smem] * 5 + [vmem] * 4,
        out_specs=(pl.BlockSpec(memory_space=pl.ANY), vmem, vmem, vmem),
        scratch_shapes=[
            pltpu.VMEM((devices, 8, HALF), F32),
            pltpu.SemaphoreType.DMA((2,)),
        ],
        name="push",
    )(cross, xself, yself, x_sizes, y_sizes, x, y, x_mass, y_mass)


def split2(value):
    high = value.astype(BF16)
    return high, (value - high.astype(F32)).astype(BF16)


def split3(value):
    high = value.astype(BF16).astype(F32)
    rest = value - high
    middle = rest.astype(BF16).astype(F32)
    return high, middle, rest - middle


def left_kernel(x_ref, y_ref, left_ref):
    for side, points in enumerate((x_ref, y_ref)):
        for c in range(CL):
            scaled = points[:, c * CS : (c + 1) * CS] * (LOG2E / EPSILON)
            turned = jnp.transpose(jnp.concatenate([scaled, scaled], axis=0))
            high = turned.astype(BF16).astype(F32)
            low = turned - high
            left_ref[side * CL + c, :, 0:HALF] = high.astype(BF16)
            lane = lax.broadcasted_iota(jnp.int32, (CS, HALF), 1)
            left_ref[side * CL + c, :, HALF:CS] = jnp.where(lane < D, low, 0.0).astype(BF16)


def left_side(x, y):
    vmem = pl.BlockSpec(memory_space=pltpu.VMEM)
    return pl.pallas_call(
        left_kernel,
        out_shape=jax.ShapeDtypeStruct((2 * CL, CS, CS), BF16),
        in_specs=[vmem, vmem],
        out_specs=vmem,
        name="left_side",
    )(x, y)


def tile_kernel(first, *refs):
    if first:
        (codes, moved, x_ref, y_ref, left, bias, back, log_cols, log_own,
         held, left2, acc, top, sums, own, count, slots, targets, rows, state, sems) = refs
        message = None
    else:
        (codes, moved, message, x_ref, y_ref, left, bias, back, log_cols, log_own,
         held, left2, acc, top, sums, own, count, slots, targets, rows, state, sems) = refs
    devices = moved.shape[0]
    pieces = sems.shape[0]
    step = devices // pieces

    def fetch(i):
        part = pl.ds(i * step, step)
        return pltpu.make_async_copy(moved.at[part], held.at[part], sems.at[i])

    for i in range(pieces):
        fetch(i).start()

    row8 = lax.broadcasted_iota(jnp.int32, (8, HALF), 0)
    ones = jnp.where(row8 < 3, 1.0, 0.0)
    for t in range(3):
        for h in range(2):
            high, middle, low = split3(bias[pl.ds((t + 1) * 2 * CL + h, CL, stride=2), :])
            stack = jnp.concatenate(
                [jnp.zeros((D, HALF), F32), high, middle, low, ones, jnp.zeros((32, HALF), F32)], axis=0
            )
            turned = jnp.transpose(stack).astype(BF16)
            for e in range(CL):
                cluster = e if t == 1 else CL + e
                here = pl.ds(h * HALF, HALF)
                left2[t * CL + e, here, :] = left[cluster, here, pl.ds(HALF, HALF)] + turned

    def clear(te, _):
        count[te] = 1
        return 0

    lax.fori_loop(0, 3 * CL, clear, 0)

    def gather(s, n):
        code = codes[s]

        @pl.when(code > 0)
        def _():
            slots[n] = s
            targets[n] = code - 1
            rows[n] = 2 * s

        return n + (code > 0).astype(jnp.int32)

    live = lax.fori_loop(0, devices, gather, 0)
    for i in range(GROUP - 1):
        slots[live + i] = slots[0]
        targets[live + i] = 0
        rows[live + i] = 2 * devices

    def scores(coords, a, te, e, cluster):
        high, low = split2(coords)
        a1, a2, a3 = split3(a)
        row = lax.broadcasted_iota(jnp.int32, (8, CS), 0)
        pick = jnp.where(row == e, 1.0, 0.0)
        mine = jnp.where(row == 0, a1, jnp.where(row == 1, a2, jnp.where(row == 2, a3, 0.0)))
        tail = jnp.concatenate([pick, pick, pick, mine], axis=0).astype(BF16)
        right = jnp.concatenate([high, low, high, tail, jnp.zeros((32, CS), BF16)], axis=0)
        return jnp.dot(
            jnp.concatenate([left[cluster, :, 0:HALF], left2[te]], axis=1),
            right,
            preferred_element_type=F32,
        )

    def fast(z, a, te, out, at):
        value = jnp.exp2(z)
        row_sum = jnp.where(a > REAL, jnp.sum(value, axis=0, keepdims=True), 1.0)
        out[pl.ds(at, 1), :] = row_sum[:, 0:HALF]
        out[pl.ds(at + 1, 1), :] = row_sum[:, HALF:CS]
        acc[te] = acc[te] + (value[:, 0:HALF] + value[:, HALF:CS])

    def slow(z, a, te, out, at):
        peak = jnp.max(z, axis=0, keepdims=True)
        total = jnp.sum(jnp.exp2(z - peak), axis=0, keepdims=True)
        log_sum = peak + jnp.log(total) * LOG2E
        out[pl.ds(at, 1), :] = log_sum[:, 0:HALF]
        out[pl.ds(at + 1, 1), :] = log_sum[:, HALF:CS]
        peak = jnp.max(z, axis=1, keepdims=True)
        total = jnp.sum(jnp.exp2(z - peak), axis=1, keepdims=True)
        before = top[te]
        now = jnp.maximum(before, peak)
        acc[te] = acc[te] * jnp.exp2(before - now) + total * jnp.exp2(peak - now)
        top[te] = now

    def sweep_local(finish):
        for t in range(3):
            points = y_ref if t == 2 else x_ref
            base = (0, 2, 3)[t] * 2 * CL

            def one(e, _):
                at = base + 2 * e
                a = jnp.concatenate([bias[pl.ds(at, 1), :], bias[pl.ds(at + 1, 1), :]], axis=1)
                z = scores(
                    points[:, pl.ds(pl.multiple_of(e * CS, CS), CS)], a, t * CL + e, e,
                    e if t == 1 else CL + e,
                )
                finish(z, a, t * CL + e, own, t * 2 * CL + 2 * e)
                return 0

            lax.fori_loop(0, CL, one, 0)

    def sweep_moved(finish):
        def some(i, _):
            for j in range(GROUP):
                n = i * GROUP + j
                s, te, at = slots[n], targets[n], rows[n]
                e = te % CL
                cluster = jnp.where(te // CL == 1, e, CL + e)
                coords = jnp.concatenate([held[s, 0:D, :], held[s, D : 2 * D, :]], axis=1)
                if first:
                    a = jnp.concatenate(
                        [held[s, 2 * D : 2 * D + 1, :], held[s, 2 * D + 1 : 2 * D + 2, :]], axis=1
                    )
                else:
                    a = jnp.concatenate(
                        [message[pl.ds(2 * s, 1), :], message[pl.ds(2 * s + 1, 1), :]], axis=1
                    )
                a = jnp.where(at < 2 * devices, a, LOG2E * NEGATIVE)
                finish(scores(coords, a, te, e, cluster), a, te, sums, at)
            return 0

        lax.fori_loop(0, pl.cdiv(live, GROUP), some, 0)

    def columns(log_domain):
        lane = lax.broadcasted_iota(jnp.int32, (CS, HALF), 1)

        def one(te, packed):
            if log_domain:
                value = jnp.max(top[te] + jnp.log(acc[te]) * LOG2E, axis=1, keepdims=True)
            else:
                value = jnp.sum(acc[te], axis=1, keepdims=True)
            return jnp.where(lane == te, value, packed)

        packed = lax.fori_loop(0, 3 * CL, one, jnp.zeros((CS, HALF), F32))
        for h in range(2):
            turned = jnp.transpose(packed[h * HALF : (h + 1) * HALF, :])
            for t in range(3):
                log_cols[pl.ds(t * 2 * CL + h, CL, stride=2), :] = turned[t * CL : (t + 1) * CL, :]

    acc[...] = jnp.zeros_like(acc)
    sums[...] = jnp.ones_like(sums)
    sweep_local(fast)
    for i in range(pieces):
        fetch(i).wait()
    sweep_moved(fast)
    columns(False)
    col = log_cols[...]
    real = bias[2 * CL : 8 * CL, :] > REAL
    col_ok = jnp.where(real, col, 1.0)
    lowest = jnp.minimum(jnp.min(sums[...]), jnp.minimum(jnp.min(own[...]), jnp.min(col_ok)))
    highest = jnp.maximum(jnp.max(sums[...]), jnp.maximum(jnp.max(own[...]), jnp.max(col_ok)))
    within = jnp.logical_and(lowest > TINY, highest < HUGE)

    @pl.when(within)
    def _():
        back[...] = jnp.log(sums[0 : 2 * devices, :]) * LOG2E
        log_own[...] = jnp.log(own[0 : 2 * CL, :]) * LOG2E
        log_cols[...] = jnp.log(col_ok) * LOG2E

    @pl.when(jnp.logical_not(within))
    def _():
        acc[...] = jnp.zeros_like(acc)
        top[...] = jnp.full_like(top, 3.0 * NEGATIVE)
        sweep_local(slow)
        sweep_moved(slow)
        columns(True)
        back[...] = sums[0 : 2 * devices, :]
        log_own[...] = own[0 : 2 * CL, :]


def tiles(codes, moved, message, x, y, left, bias):
    first = message is None
    devices = moved.shape[0]
    smem = pl.BlockSpec(memory_space=pltpu.SMEM)
    vmem = pl.BlockSpec(memory_space=pltpu.VMEM)
    hbm = pl.BlockSpec(memory_space=pl.ANY)
    args = (codes, moved) + (() if first else (message,)) + (x, y, left, bias)
    return pl.pallas_call(
        functools.partial(tile_kernel, first),
        out_shape=(
            jax.ShapeDtypeStruct((2 * devices, HALF), F32),
            jax.ShapeDtypeStruct((6 * CL, HALF), F32),
            jax.ShapeDtypeStruct((2 * CL, HALF), F32),
        ),
        in_specs=[smem, hbm] + [vmem] * (4 if first else 5),
        out_specs=(vmem, vmem, vmem),
        scratch_shapes=[
            pltpu.VMEM((devices, ROWS, HALF), F32),
            pltpu.VMEM((3 * CL, CS, HALF), BF16),
            pltpu.VMEM((3 * CL, CS, HALF), F32),
            pltpu.VMEM((3 * CL, CS, HALF), F32),
            pltpu.VMEM((2 * devices + 8, HALF), F32),
            pltpu.VMEM((6 * CL, HALF), F32),
            pltpu.SMEM((3 * CL,), jnp.int32),
            pltpu.SMEM((devices + GROUP,), jnp.int32),
            pltpu.SMEM((devices + GROUP,), jnp.int32),
            pltpu.SMEM((devices + GROUP,), jnp.int32),
            pltpu.SMEM((1,), jnp.int32),
            pltpu.SemaphoreType.DMA((16,)),
        ],
        name="tiles_first" if first else "tiles",
    )(*args)


def log_sum(values):
    peak = functools.reduce(jnp.maximum, values)
    total = functools.reduce(jnp.add, [jnp.exp2(value - peak) for value in values])
    return peak + jnp.log(total) * LOG2E


def update_kernel(
    last, cross, xself, yself, back, log_cols, log_own, weight, half, potential, bias, *refs
):
    if last:
        new, parts = refs
    else:
        new, new_bias, message, parts = refs
    counts = (cross.shape[1], xself.shape[1], yself.shape[1])
    offsets = (0, counts[0], counts[0] + counts[1])
    requests = list(lists(cross, xself, yself))
    for kind, c, k, named in requests:
        at = pl.multiple_of(2 * (named // CL), 2)
        parts[offsets[kind] + k, 2 * c : 2 * c + 2, :] = back[pl.ds(at, 2), :]
    span = 2 * CL
    answers = [[parts[offsets[t] + k] for k in range(counts[t])] for t in range(3)]
    totals = (
        log_sum([log_own[...]] + answers[0]),
        log_cols[0:span, :],
        log_sum([log_cols[span : 2 * span, :]] + answers[1]),
        log_sum([log_cols[2 * span : 3 * span, :]] + answers[2]),
    )
    for i, total in enumerate(totals):
        here = slice(i * span, (i + 1) * span)
        side = slice((i % 2) * span, (i % 2 + 1) * span)
        log_total = LN2 * (total - bias[here, :]) - half[side, :] / EPSILON
        fresh = 0.5 * (potential[here, :] - DAMPING * EPSILON * log_total)
        fresh = jnp.where(weight[side, :] > REAL, fresh, 0.0)
        new[here, :] = fresh
        if not last:
            new_bias[here, :] = bias_of(weight[side, :], half[side, :], fresh)
    if last:
        return
    for kind, c, _, named in requests:
        at = pl.multiple_of(2 * (named // CL), 2)
        base = (0, 2 * span, 3 * span)[kind] + 2 * c
        message[pl.ds(at, 2), :] = new_bias[base : base + 2, :]


def update(last, cross, xself, yself, back, log_cols, log_own, weight, half, potential, bias):
    smem = pl.BlockSpec(memory_space=pltpu.SMEM)
    vmem = pl.BlockSpec(memory_space=pltpu.VMEM)
    small = jax.ShapeDtypeStruct((8 * CL, HALF), F32)
    shapes = (small,) if last else (small, small, jax.ShapeDtypeStruct(back.shape, F32))
    listed = cross.shape[1] + xself.shape[1] + yself.shape[1]
    return pl.pallas_call(
        functools.partial(update_kernel, last),
        out_shape=shapes,
        in_specs=[smem] * 3 + [vmem] * 7,
        out_specs=(vmem,) * len(shapes),
        scratch_shapes=[pltpu.VMEM((listed, 2 * CL, HALF), F32)],
        name="update",
    )(cross, xself, yself, back, log_cols, log_own, weight, half, potential, bias)


def exchange(blocks):
    return lax.all_to_all(blocks, AXES, split_axis=0, concat_axis=0, tiled=True)


def exchange_rows(rows, devices):
    return exchange(rows.reshape(devices, 2, HALF)).reshape(2 * devices, HALF)


def local(x, y, x_logmass, y_logmass, x_sizes, y_sizes, cross, xself, yself):
    devices = lax.axis_size(AXES)
    send, weight, half, bias = push(
        cross, xself, yself, x_sizes, y_sizes, x, y,
        x_logmass.reshape(2 * CL, HALF), y_logmass.reshape(2 * CL, HALF), devices,
    )
    moved = exchange(send)
    left = left_side(x, y)
    codes = moved[:, 2 * D + 2, 0].astype(jnp.int32)
    potential = jnp.zeros((8 * CL, HALF), F32)
    message = None
    for iteration in range(ITERS):
        last = iteration == ITERS - 1
        back, log_cols, log_own = tiles(codes, moved, message, x, y, left, bias)
        back = exchange_rows(back, devices)
        out = update(last, cross, xself, yself, back, log_cols, log_own, weight, half, potential, bias)
        if last:
            (potential,) = out
        else:
            potential, bias, message = out
            message = exchange_rows(message, devices)
    parts = potential.reshape(4, 2 * CL * HALF)
    return parts[0], parts[1], parts[2], parts[3]


def solution(mesh):
    flat, table = P(AXES), P(AXES, None)
    points = P(None, AXES)
    return jax.shard_map(
        local,
        mesh=mesh,
        in_specs=(points, points, flat, flat, table, table, table, table, table),
        out_specs=(flat, flat, flat, flat),
        check_vma=False,
    )
```

```python
import functools

import jax
import jax.numpy as jnp
from jax import lax
from jax.experimental import pallas as pl
from jax.experimental.pallas import tpu as pltpu
from jax.sharding import PartitionSpec as P

ITERS = 3
EPSILON = 0.5
DAMPING = 2.0 / (2.0 + 0.5)
NEGATIVE = -1e30
REAL = -1e29
LOG2E = 1.4426950408889634
LN2 = 0.6931471805599453
TINY = 2.0**-90
HUGE = 2.0**90
AXES = ("row", "col")

D = 64
CS = 256
CL = 8
HALF = 128
ROWS = 2 * D + 8
GROUP = 8
LOCAL_GROUP = 4
PIECES = 8
BF16 = jnp.bfloat16
F32 = jnp.float32


def lists(cross, xself, yself):
    for c in range(cross.shape[0]):
        for k in range(cross.shape[1]):
            yield 0, c, k, cross[c, k]
    for table, kind in ((xself, 1), (yself, 2)):
        for c in range(table.shape[1]):
            for k in range(table.shape[0]):
                yield kind, c, k, table[k, c]


def bias_of(weight, half, potential):
    return LOG2E * (weight + (potential - half) / EPSILON)


def push_kernel(
    cross, xself, yself, x_sizes, y_sizes, x_ref, y_ref, x_mass, y_mass,
    send, weight_ref, half_ref, bias_g_ref, bias_ref, aux, sems,
):
    devices = send.shape[0]
    requests = list(lists(cross, xself, yself))
    for kind, c, _, named in requests:
        owner = named // CL
        source = y_ref if kind == 2 else x_ref
        for h in range(2):
            pltpu.make_async_copy(
                source.at[:, pl.ds(c * CS + h * HALF, HALF)],
                send.at[owner, pl.ds(h * D, D), :],
                sems.at[0],
            ).start()
    row = lax.broadcasted_iota(jnp.int32, (2 * CL, HALF), 0)
    position = (row % 2) * HALF + lax.broadcasted_iota(jnp.int32, (2 * CL, HALF), 1)
    for side, (points, sizes, mass) in enumerate(
        ((x_ref, x_sizes, x_mass), (y_ref, y_sizes, y_mass))
    ):
        count = jnp.zeros((2 * CL, HALF), jnp.int32)
        for c in range(CL):
            count = jnp.where(row // 2 == c, sizes[0, c], count)
        base = side * 2 * CL
        weight_ref[base : base + 2 * CL, :] = jnp.where(position < count, mass[...], NEGATIVE)
        for t in range(2 * CL):
            piece = points[:, t * HALF : (t + 1) * HALF]
            half_ref[base + t : base + t + 1, :] = 0.5 * jnp.sum(piece * piece, axis=0, keepdims=True)
    bias = bias_of(weight_ref[...], half_ref[...], 0.0)
    bias_ref[0 : 2 * CL, :] = bias[0 : 2 * CL, :]
    bias_ref[2 * CL : 6 * CL, :] = bias
    bias_g_ref[...] = bias[2 * CL : 4 * CL, :]
    aux[...] = jnp.zeros_like(aux)
    for kind, c, _, named in requests:
        owner = named // CL
        base = kind * 2 * CL + 2 * c
        aux[owner, 0:2, :] = bias_ref[base : base + 2, :]
        code = (kind * CL + named % CL + 1).astype(F32)
        aux[owner, 2:3, :] = jnp.full((1, HALF), code, F32)
    tail = pltpu.make_async_copy(aux, send.at[:, pl.ds(2 * D, 8), :], sems.at[1])
    tail.start()
    tail.wait()
    sent = send.at[pl.ds(0, len(requests)), pl.ds(0, 2 * D), :]
    pltpu.make_async_copy(sent, sent, sems.at[0]).wait()


def push(cross, xself, yself, x_sizes, y_sizes, x, y, x_mass, y_mass, devices):
    smem = pl.BlockSpec(memory_space=pltpu.SMEM)
    vmem = pl.BlockSpec(memory_space=pltpu.VMEM)
    return pl.pallas_call(
        push_kernel,
        out_shape=(
            jax.ShapeDtypeStruct((devices, ROWS, HALF), F32),
            jax.ShapeDtypeStruct((4 * CL, HALF), F32),
            jax.ShapeDtypeStruct((4 * CL, HALF), F32),
            jax.ShapeDtypeStruct((2 * CL, HALF), F32),
            jax.ShapeDtypeStruct((6 * CL, HALF), F32),
        ),
        in_specs=[smem] * 5 + [vmem] * 4,
        out_specs=(pl.BlockSpec(memory_space=pl.ANY), vmem, vmem, vmem, vmem),
        scratch_shapes=[
            pltpu.VMEM((devices, 8, HALF), F32),
            pltpu.SemaphoreType.DMA((2,)),
        ],
        name="push",
    )(cross, xself, yself, x_sizes, y_sizes, x, y, x_mass, y_mass)


def split2(value):
    high = value.astype(BF16)
    return high, (value - high.astype(F32)).astype(BF16)


def split3(value):
    high = value.astype(BF16).astype(F32)
    rest = value - high
    middle = rest.astype(BF16).astype(F32)
    return high, middle, rest - middle


def left_kernel(x_ref, y_ref, left_ref, right_ref):
    lane = lax.broadcasted_iota(jnp.int32, (CS, HALF), 1)
    for side, points in enumerate((x_ref, y_ref)):
        for c in range(CL):
            piece = points[:, c * CS : (c + 1) * CS]
            scaled = piece * (LOG2E / EPSILON)
            turned = jnp.transpose(jnp.concatenate([scaled, scaled], axis=0))
            high, low = split2(turned)
            left_ref[side * CL + c, :, 0:HALF] = high
            low = jnp.where(lane < D, low.astype(F32), 0.0)
            left_ref[side * CL + c, :, HALF:CS] = low.astype(BF16)
            high, low = split2(piece)
            right_ref[side * CL + c, 0:D, :] = high
            right_ref[side * CL + c, D:HALF, :] = low


def left_side(x, y):
    vmem = pl.BlockSpec(memory_space=pltpu.VMEM)
    return pl.pallas_call(
        left_kernel,
        out_shape=(
            jax.ShapeDtypeStruct((2 * CL, CS, CS), BF16),
            jax.ShapeDtypeStruct((2 * CL, HALF, CS), BF16),
        ),
        in_specs=[vmem, vmem],
        out_specs=(vmem, vmem),
        name="left_side",
    )(x, y)


def scores(left_high, left_rest, high, low, a, e):
    a1, a2, a3 = split3(a)
    row = lax.broadcasted_iota(jnp.int32, (8, CS), 0)
    pick = jnp.where(row == e, 1.0, 0.0)
    mine = jnp.where(row == 0, a1, jnp.where(row == 1, a2, jnp.where(row == 2, a3, 0.0)))
    tail = jnp.concatenate([pick, pick, pick, mine], axis=0).astype(BF16)
    right = jnp.concatenate([high, low, high, tail, jnp.zeros((32, CS), BF16)], axis=0)
    return jnp.dot(
        jnp.concatenate([left_high, left_rest], axis=1), right, preferred_element_type=F32
    )


def put_row(out, at, value):
    out[pl.ds(at, 1), :] = value[:, 0:HALF]
    out[pl.ds(at + 1, 1), :] = value[:, HALF:CS]


def row_sum(value, a):
    return jnp.where(a > REAL, jnp.sum(value, axis=0, keepdims=True), 1.0)


def fold(value):
    return value[:, 0:HALF] + value[:, HALF:CS]


def row_log_sum(z):
    peak = jnp.max(z, axis=0, keepdims=True)
    total = jnp.sum(jnp.exp2(z - peak), axis=0, keepdims=True)
    return peak + jnp.log(total) * LOG2E


def merge_columns(z, te, acc, top):
    peak = jnp.max(z, axis=1, keepdims=True)
    total = jnp.sum(jnp.exp2(z - peak), axis=1, keepdims=True)
    before = top[te]
    now = jnp.maximum(before, peak)
    acc[te] = acc[te] * jnp.exp2(before - now) + total * jnp.exp2(peak - now)
    top[te] = now


def columns(acc, top, cols):
    lane = lax.broadcasted_iota(jnp.int32, (CS, HALF), 1)
    batch = 1 if top is not None else 8

    def some(i, packed):
        for j in range(batch):
            te = i * batch + j
            if top is not None:
                value = jnp.max(top[te] + jnp.log(acc[te]) * LOG2E, axis=1, keepdims=True)
            else:
                value = jnp.sum(acc[te], axis=1, keepdims=True)
            packed = jnp.where(lane == te, value, packed)
        return packed

    packed = lax.fori_loop(0, 3 * CL // batch, some, jnp.zeros((CS, HALF), F32))
    for h in range(2):
        turned = jnp.transpose(packed[h * HALF : (h + 1) * HALF, :])
        for t in range(3):
            cols[pl.ds(t * 2 * CL + h, CL, stride=2), :] = turned[t * CL : (t + 1) * CL, :]


def in_range(*values):
    lowest = functools.reduce(jnp.minimum, [jnp.min(value) for value in values])
    highest = functools.reduce(jnp.maximum, [jnp.max(value) for value in values])
    return jnp.logical_and(lowest > TINY, highest < HUGE)


def local_kernel(left, right, bias_g, bias, left2, log_cols, log_own, acc, top, own):
    row8 = lax.broadcasted_iota(jnp.int32, (8, HALF), 0)
    ones = jnp.where(row8 < 3, 1.0, 0.0)
    span = 2 * CL
    for t in range(3):
        for h in range(2):
            if t == 0:
                value = bias_g[pl.ds(h, CL, stride=2), :]
            else:
                value = bias[pl.ds(t * span + h, CL, stride=2), :]
            high, middle, low = split3(value)
            stack = jnp.concatenate(
                [jnp.zeros((D, HALF), F32), high, middle, low, ones, jnp.zeros((32, HALF), F32)], axis=0
            )
            turned = jnp.transpose(stack).astype(BF16)
            for e in range(CL):
                cluster = e if t == 1 else CL + e
                here = pl.ds(h * HALF, HALF)
                left2[t * CL + e, here, :] = left[cluster, here, pl.ds(HALF, HALF)] + turned

    def sweep(finish):
        for t in range(3):

            def some(i, _):
                for j in range(LOCAL_GROUP):
                    e = i * LOCAL_GROUP + j
                    at = t * span + 2 * e
                    a = jnp.concatenate([bias[pl.ds(at, 1), :], bias[pl.ds(at + 1, 1), :]], axis=1)
                    source = CL + e if t == 2 else e
                    z = scores(
                        left[e if t == 1 else CL + e, :, 0:HALF], left2[t * CL + e],
                        right[source, 0:D, :], right[source, D:HALF, :], a, e,
                    )
                    finish(z, a, t, e)
                return 0

            lax.fori_loop(0, CL // LOCAL_GROUP, some, 0)

    def fast(z, a, t, e):
        value = jnp.exp2(z)
        if t == 0:
            put_row(own, 2 * e, row_sum(value, a))
        acc[t * CL + e] = fold(value)

    def slow(z, a, t, e):
        if t == 0:
            put_row(own, 2 * e, row_log_sum(z))
        merge_columns(z, t * CL + e, acc, top)

    sweep(fast)
    columns(acc, None, log_cols)
    real = jnp.concatenate([bias_g[...], bias[span : 3 * span, :]], axis=0) > REAL
    cols = jnp.where(real, log_cols[...], 1.0)
    within = in_range(own[...], cols)

    @pl.when(within)
    def _():
        log_own[...] = jnp.log(own[...]) * LOG2E
        log_cols[...] = jnp.log(cols) * LOG2E

    @pl.when(jnp.logical_not(within))
    def _():
        acc[...] = jnp.zeros_like(acc)
        top[...] = jnp.full_like(top, 3.0 * NEGATIVE)
        sweep(slow)
        columns(acc, top, log_cols)
        log_own[...] = own[...]


def local_tiles(left, right, bias_g, bias):
    vmem = pl.BlockSpec(memory_space=pltpu.VMEM)
    return pl.pallas_call(
        local_kernel,
        out_shape=(
            jax.ShapeDtypeStruct((3 * CL, CS, HALF), BF16),
            jax.ShapeDtypeStruct((6 * CL, HALF), F32),
            jax.ShapeDtypeStruct((2 * CL, HALF), F32),
        ),
        in_specs=[vmem] * 4,
        out_specs=(vmem,) * 3,
        scratch_shapes=[
            pltpu.VMEM((3 * CL, CS, HALF), F32),
            pltpu.VMEM((3 * CL, CS, HALF), F32),
            pltpu.VMEM((2 * CL, HALF), F32),
        ],
        name="local_tiles",
    )(left, right, bias_g, bias)


def tile_kernel(first, *refs):
    if first:
        (moved, left, left2, bias_g, bias, back, log_cols, slots, targets, bounds, listed,
         held, acc, top, sums, codes, count, sems) = refs
        message = None
    else:
        (moved, message, left, left2, bias_g, bias, slots, targets, bounds, listed,
         back, log_cols, held, acc, top, sums, sems) = refs
    devices = moved.shape[0]
    step = devices // PIECES

    def fetch(i):
        part = pl.ds(i * step, step)
        return pltpu.make_async_copy(moved.at[part], held.at[part], sems.at[i])

    if first:
        tags = pltpu.make_async_copy(moved.at[:, pl.ds(2 * D + 2, 1), :], codes, sems.at[PIECES])
        tags.start()
    for i in range(PIECES):
        fetch(i).start()
    acc[...] = jnp.zeros_like(acc)
    sums[...] = jnp.ones_like(sums)
    if first:
        tags.wait()
        for te in range(3 * CL):
            count[te] = 0

        def gather(s, n):
            code = codes[s, 0, 0].astype(jnp.int32)

            @pl.when(code > 0)
            def _():
                slots[n] = s
                targets[n] = code - 1
                count[code - 1] = 1

            n = n + (code > 0).astype(jnp.int32)
            bounds[s] = n
            return n

        lax.fori_loop(0, devices, gather, 0, unroll=8)
        row = lax.broadcasted_iota(jnp.int32, listed.shape, 0) // 2
        some_listed = jnp.zeros(listed.shape, jnp.int32)
        for te in range(3 * CL):
            some_listed = jnp.where(row == te, count[te], some_listed)
        listed[...] = some_listed
    live = bounds[devices - 1]
    if first:
        for i in range(GROUP):
            slots[live + i] = slots[0]
            targets[live + i] = 0

    def group(finish):
        def run(i, _):
            for j in range(GROUP):
                n = i * GROUP + j
                s, te = slots[n], targets[n]
                e = te % CL
                cluster = jnp.where(te // CL == 1, e, CL + e)
                at = jnp.where(n < live, 2 * s, 2 * devices)
                high, low = split2(jnp.concatenate([held[s, 0:D, :], held[s, D : 2 * D, :]], axis=1))
                if first:
                    pair = held[s, 2 * D : 2 * D + 1, :], held[s, 2 * D + 1 : 2 * D + 2, :]
                else:
                    pair = message[pl.ds(2 * s, 1), :], message[pl.ds(2 * s + 1, 1), :]
                a = jnp.where(n < live, jnp.concatenate(pair, axis=1), LOG2E * NEGATIVE)
                z = scores(left[cluster, :, 0:HALF], left2[te], high, low, a, e)
                finish(z, a, te, at)
            return 0

        return run

    def fast(z, a, te, at):
        value = jnp.exp2(z)
        put_row(sums, at, row_sum(value, a))
        acc[te] = acc[te] + fold(value)

    def slow(z, a, te, at):
        put_row(sums, at, row_log_sum(z))
        merge_columns(z, te, acc, top)

    def piece(i, start):
        fetch(i).wait()
        ready = bounds[(i + 1) * step - 1]
        stop = jnp.where(i == PIECES - 1, (live + GROUP - 1) // GROUP, ready // GROUP)
        lax.fori_loop(start, stop, group(fast), 0)
        return stop

    lax.fori_loop(0, PIECES, piece, 0)
    columns(acc, None, log_cols)
    real = jnp.concatenate([bias_g[...], bias[2 * CL : 6 * CL, :]], axis=0) > REAL
    named = listed[...] > 0
    cols = jnp.where(jnp.logical_and(real, named), log_cols[...], 1.0)
    within = in_range(sums[...], cols)

    @pl.when(within)
    def _():
        back[...] = jnp.log(sums[0 : 2 * devices, :]) * LOG2E
        log_cols[...] = jnp.where(named, jnp.log(cols) * LOG2E, NEGATIVE)

    @pl.when(jnp.logical_not(within))
    def _():
        acc[...] = jnp.zeros_like(acc)
        top[...] = jnp.full_like(top, 3.0 * NEGATIVE)
        lax.fori_loop(0, (live + GROUP - 1) // GROUP, group(slow), 0)
        columns(acc, top, log_cols)
        log_cols[...] = jnp.where(named, log_cols[...], NEGATIVE)
        back[...] = sums[0 : 2 * devices, :]


def tiles(moved, message, left, left2, bias_g, bias, index):
    first = index is None
    devices = moved.shape[0]
    smem = pl.BlockSpec(memory_space=pltpu.SMEM)
    vmem = pl.BlockSpec(memory_space=pltpu.VMEM)
    hbm = pl.BlockSpec(memory_space=pl.ANY)
    outs = [
        jax.ShapeDtypeStruct((2 * devices, HALF), F32),
        jax.ShapeDtypeStruct((6 * CL, HALF), F32),
    ]
    index_shapes = [
        jax.ShapeDtypeStruct((devices + GROUP,), jnp.int32),
        jax.ShapeDtypeStruct((devices + GROUP,), jnp.int32),
        jax.ShapeDtypeStruct((devices,), jnp.int32),
        jax.ShapeDtypeStruct((6 * CL, HALF), jnp.int32),
    ]
    index_specs = [smem, smem, smem, vmem]
    scratch = [
        pltpu.VMEM((devices, ROWS, HALF), F32),
        pltpu.VMEM((3 * CL, CS, HALF), F32),
        pltpu.VMEM((3 * CL, CS, HALF), F32),
        pltpu.VMEM((2 * devices + 8, HALF), F32),
    ]
    if first:
        scratch += [pltpu.SMEM((devices, 1, HALF), F32), pltpu.SMEM((3 * CL,), jnp.int32)]
    scratch += [pltpu.SemaphoreType.DMA((PIECES + 1,))]
    out = pl.pallas_call(
        functools.partial(tile_kernel, first),
        out_shape=outs + (index_shapes if first else []),
        in_specs=[hbm] + [vmem] * (4 if first else 5) + ([] if first else index_specs),
        out_specs=[vmem, vmem] + (index_specs if first else []),
        scratch_shapes=scratch,
        name="tiles_first" if first else "tiles",
    )(*((moved, left, left2, bias_g, bias) if first else (moved, message, left, left2, bias_g, bias, *index)))
    return out[0], out[1], out[2:] if first else index


def log_sum(values):
    peak = functools.reduce(jnp.maximum, values)
    total = functools.reduce(jnp.add, [jnp.exp2(value - peak) for value in values])
    return peak + jnp.log(total) * LOG2E


def fresh(total, bias, weight, half, potential):
    log_total = LN2 * (total - bias) - half / EPSILON
    value = 0.5 * (potential - DAMPING * EPSILON * log_total)
    return jnp.where(weight > REAL, value, 0.0)


def update_g_kernel(cols_local, cols_moved, weight, half, bias, potential, new, *new_bias):
    side = slice(2 * CL, 4 * CL)
    span = slice(0, 2 * CL)
    total = log_sum([cols_local[span, :], cols_moved[span, :]])
    value = fresh(total, bias[...], weight[side, :], half[side, :], potential[...])
    new[...] = value
    for ref in new_bias:
        ref[...] = bias_of(weight[side, :], half[side, :], value)


def update_g(last, *args):
    vmem = pl.BlockSpec(memory_space=pltpu.VMEM)
    shapes = (jax.ShapeDtypeStruct((2 * CL, HALF), F32),) * (1 if last else 2)
    return pl.pallas_call(
        update_g_kernel,
        out_shape=shapes,
        in_specs=[vmem] * 6,
        out_specs=(vmem,) * len(shapes),
        name="update_g",
    )(*args)


def update_kernel(
    last, cross, xself, yself, back, cols_local, cols_moved, log_own, weight, half, potential, bias, *refs
):
    if last:
        *new, parts = refs
    else:
        new, new_bias, message, parts = refs
    counts = (cross.shape[1], xself.shape[0], yself.shape[0])
    offsets = (0, counts[0], counts[0] + counts[1])
    requests = list(lists(cross, xself, yself))
    for kind, c, k, named in requests:
        at = pl.multiple_of(2 * (named // CL), 2)
        parts[offsets[kind] + k, 2 * c : 2 * c + 2, :] = back[pl.ds(at, 2), :]
    span = 2 * CL
    answers = [[parts[offsets[t] + k] for k in range(counts[t])] for t in range(3)]
    p, q = slice(span, 2 * span), slice(2 * span, 3 * span)
    totals = (
        log_sum([log_own[...]] + answers[0]),
        log_sum([cols_local[p, :], cols_moved[p, :]] + answers[1]),
        log_sum([cols_local[q, :], cols_moved[q, :]] + answers[2]),
    )
    for i, total in enumerate(totals):
        here = slice(i * span, (i + 1) * span)
        side = slice(span, 2 * span) if i == 2 else slice(0, span)
        value = fresh(total, bias[here, :], weight[side, :], half[side, :], potential[here, :])
        if last:
            new[i][...] = value
        else:
            new[here, :] = value
            new_bias[here, :] = bias_of(weight[side, :], half[side, :], value)
    if last:
        return
    for kind, c, _, named in requests:
        at = pl.multiple_of(2 * (named // CL), 2)
        base = kind * span + 2 * c
        message[pl.ds(at, 2), :] = new_bias[base : base + 2, :]


def update(last, cross, xself, yself, back, *args):
    smem = pl.BlockSpec(memory_space=pltpu.SMEM)
    vmem = pl.BlockSpec(memory_space=pltpu.VMEM)
    one = jax.ShapeDtypeStruct((2 * CL, HALF), F32)
    three = jax.ShapeDtypeStruct((6 * CL, HALF), F32)
    shapes = (one,) * 3 if last else (three, three, jax.ShapeDtypeStruct(back.shape, F32))
    listed = cross.shape[1] + xself.shape[0] + yself.shape[0]
    return pl.pallas_call(
        functools.partial(update_kernel, last),
        out_shape=shapes,
        in_specs=[smem] * 3 + [vmem] * 8,
        out_specs=(vmem,) * len(shapes),
        scratch_shapes=[pltpu.VMEM((listed, 2 * CL, HALF), F32)],
        name="update",
    )(cross, xself, yself, back, *args)


def exchange(blocks):
    return lax.all_to_all(blocks, AXES, split_axis=0, concat_axis=0, tiled=True)


def exchange_rows(rows, devices):
    return exchange(rows.reshape(devices, 2, HALF)).reshape(2 * devices, HALF)


def local(x, y, x_logmass, y_logmass, x_sizes, y_sizes, cross, xself, yself):
    devices = lax.axis_size(AXES)
    xself, yself = xself.T, yself.T
    send, weight, half, bias_g, bias = push(
        cross, xself, yself, x_sizes, y_sizes, x, y,
        x_logmass.reshape(2 * CL, HALF), y_logmass.reshape(2 * CL, HALF), devices,
    )
    moved = exchange(send)
    left, right = left_side(x, y)
    potential_g = jnp.zeros((2 * CL, HALF), F32)
    potential = jnp.zeros((6 * CL, HALF), F32)
    message = index = None
    for iteration in range(ITERS):
        last = iteration == ITERS - 1
        left2, cols_local, log_own = local_tiles(left, right, bias_g, bias)
        back, cols_moved, index = tiles(moved, message, left, left2, bias_g, bias, index)
        back = exchange_rows(back, devices)
        out_g = update_g(last, cols_local, cols_moved, weight, half, bias_g, potential_g)
        out = update(
            last, cross, xself, yself, back, cols_local, cols_moved, log_own, weight, half, potential, bias
        )
        if not last:
            potential_g, bias_g = out_g
            potential, bias, message = out
            message = exchange_rows(message, devices)
    f, p, q = out
    return tuple(part.reshape(2 * CL * HALF) for part in (f, out_g[0], p, q))


def solution(mesh):
    flat, table = P(AXES), P(AXES, None)
    points = P(None, AXES)
    return jax.shard_map(
        local,
        mesh=mesh,
        in_specs=(points, points, flat, flat, table, table, table, table, table),
        out_specs=(flat, flat, flat, flat),
        check_vma=False,
    )
```

```python
import functools

import jax
import jax.numpy as jnp
from jax import lax
from jax.experimental import pallas as pl
from jax.experimental.pallas import tpu as pltpu
from jax.sharding import PartitionSpec as P

ITERS = 3
EPSILON = 0.5
DAMPING = 2.0 / (2.0 + 0.5)
NEGATIVE = -1e30
REAL = -1e29
LOG2E = 1.4426950408889634
LN2 = 0.6931471805599453
TINY = 2.0**-90
HUGE = 2.0**90
AXES = ("row", "col")

D = 64
CS = 256
CL = 8
HALF = 128
ROWS = 2 * D + 8
GROUP = 8
LOCAL_GROUP = 4
PIECES = 8
SPAN = 16
BF16 = jnp.bfloat16
F32 = jnp.float32


def lists(cross, xself, yself):
    for c in range(cross.shape[0]):
        for k in range(cross.shape[1]):
            yield 0, c, k, cross[c, k]
    for table, kind in ((xself, 1), (yself, 2)):
        for c in range(table.shape[1]):
            for k in range(table.shape[0]):
                yield kind, c, k, table[k, c]


def bias_of(weight, half, potential):
    return LOG2E * (weight + (potential - half) / EPSILON)


def push_kernel(
    cross, xself, yself, x_sizes, y_sizes, x_ref, y_ref, x_mass, y_mass,
    send, weight_ref, half_ref, bias_g_ref, bias_ref, aux, sems,
):
    devices = send.shape[0]
    requests = list(lists(cross, xself, yself))
    for kind, c, _, named in requests:
        owner = named // CL
        source = y_ref if kind == 2 else x_ref
        for h in range(2):
            pltpu.make_async_copy(
                source.at[:, pl.ds(c * CS + h * HALF, HALF)],
                send.at[owner, pl.ds(h * D, D), :],
                sems.at[0],
            ).start()
    row = lax.broadcasted_iota(jnp.int32, (2 * CL, HALF), 0)
    position = (row % 2) * HALF + lax.broadcasted_iota(jnp.int32, (2 * CL, HALF), 1)
    for side, (points, sizes, mass) in enumerate(
        ((x_ref, x_sizes, x_mass), (y_ref, y_sizes, y_mass))
    ):
        count = jnp.zeros((2 * CL, HALF), jnp.int32)
        for c in range(CL):
            count = jnp.where(row // 2 == c, sizes[0, c], count)
        base = side * 2 * CL
        weight_ref[base : base + 2 * CL, :] = jnp.where(position < count, mass[...], NEGATIVE)
        for t in range(2 * CL):
            piece = points[:, t * HALF : (t + 1) * HALF]
            half_ref[base + t : base + t + 1, :] = 0.5 * jnp.sum(piece * piece, axis=0, keepdims=True)
    bias = bias_of(weight_ref[...], half_ref[...], 0.0)
    bias_ref[0 : 2 * CL, :] = bias[0 : 2 * CL, :]
    bias_ref[2 * CL : 6 * CL, :] = bias
    bias_g_ref[...] = bias[2 * CL : 4 * CL, :]
    aux[...] = jnp.zeros_like(aux)
    for kind, c, _, named in requests:
        owner = named // CL
        base = kind * 2 * CL + 2 * c
        aux[owner, 0:2, :] = bias_ref[base : base + 2, :]
        code = (kind * CL + named % CL + 1).astype(F32)
        aux[owner, 2:3, :] = jnp.full((1, HALF), code, F32)
    tail = pltpu.make_async_copy(aux, send.at[:, pl.ds(2 * D, 8), :], sems.at[1])
    tail.start()
    tail.wait()
    sent = send.at[pl.ds(0, len(requests)), pl.ds(0, 2 * D), :]
    pltpu.make_async_copy(sent, sent, sems.at[0]).wait()


def push(cross, xself, yself, x_sizes, y_sizes, x, y, x_mass, y_mass, devices):
    smem = pl.BlockSpec(memory_space=pltpu.SMEM)
    vmem = pl.BlockSpec(memory_space=pltpu.VMEM)
    return pl.pallas_call(
        push_kernel,
        out_shape=(
            jax.ShapeDtypeStruct((devices, ROWS, HALF), F32),
            jax.ShapeDtypeStruct((4 * CL, HALF), F32),
            jax.ShapeDtypeStruct((4 * CL, HALF), F32),
            jax.ShapeDtypeStruct((2 * CL, HALF), F32),
            jax.ShapeDtypeStruct((6 * CL, HALF), F32),
        ),
        in_specs=[smem] * 5 + [vmem] * 4,
        out_specs=(pl.BlockSpec(memory_space=pl.ANY), vmem, vmem, vmem, vmem),
        scratch_shapes=[
            pltpu.VMEM((devices, 8, HALF), F32),
            pltpu.SemaphoreType.DMA((2,)),
        ],
        name="push",
    )(cross, xself, yself, x_sizes, y_sizes, x, y, x_mass, y_mass)


def split2(value):
    high = value.astype(BF16)
    return high, (value - high.astype(F32)).astype(BF16)


def split3(value):
    high = value.astype(BF16).astype(F32)
    rest = value - high
    middle = rest.astype(BF16).astype(F32)
    return high, middle, rest - middle


def left_kernel(x_ref, y_ref, left_ref, right_ref):
    lane = lax.broadcasted_iota(jnp.int32, (CS, HALF), 1)
    for side, points in enumerate((x_ref, y_ref)):
        for c in range(CL):
            piece = points[:, c * CS : (c + 1) * CS]
            scaled = piece * (LOG2E / EPSILON)
            turned = jnp.transpose(jnp.concatenate([scaled, scaled], axis=0))
            high, low = split2(turned)
            left_ref[side * CL + c, :, 0:HALF] = high
            low = jnp.where(lane < D, low.astype(F32), 0.0)
            left_ref[side * CL + c, :, HALF:CS] = low.astype(BF16)
            high, low = split2(piece)
            right_ref[side * CL + c, 0:D, :] = high
            right_ref[side * CL + c, D:HALF, :] = low


def left_side(x, y):
    vmem = pl.BlockSpec(memory_space=pltpu.VMEM)
    return pl.pallas_call(
        left_kernel,
        out_shape=(
            jax.ShapeDtypeStruct((2 * CL, CS, CS), BF16),
            jax.ShapeDtypeStruct((2 * CL, HALF, CS), BF16),
        ),
        in_specs=[vmem, vmem],
        out_specs=(vmem, vmem),
        name="left_side",
    )(x, y)


def scores(left_high, left_rest, high, low, a, e):
    a1, a2, a3 = split3(a)
    row = lax.broadcasted_iota(jnp.int32, (8, CS), 0)
    pick = jnp.where(row == e, 1.0, 0.0)
    mine = jnp.where(row == 0, a1, jnp.where(row == 1, a2, jnp.where(row == 2, a3, 0.0)))
    tail = jnp.concatenate([pick, pick, pick, mine], axis=0).astype(BF16)
    right = jnp.concatenate([high, low, high, tail, jnp.zeros((32, CS), BF16)], axis=0)
    return jnp.dot(
        jnp.concatenate([left_high, left_rest], axis=1), right, preferred_element_type=F32
    )


def put_row(out, at, value):
    out[pl.ds(at, 1), :] = value[:, 0:HALF]
    out[pl.ds(at + 1, 1), :] = value[:, HALF:CS]


def row_sum(value, a):
    return jnp.where(a > REAL, jnp.sum(value, axis=0, keepdims=True), 1.0)


def fold(value):
    return value[:, 0:HALF] + value[:, HALF:CS]


def row_log_sum(z):
    peak = jnp.max(z, axis=0, keepdims=True)
    total = jnp.sum(jnp.exp2(z - peak), axis=0, keepdims=True)
    return peak + jnp.log(total) * LOG2E


def merge_columns(z, te, acc, top):
    peak = jnp.max(z, axis=1, keepdims=True)
    total = jnp.sum(jnp.exp2(z - peak), axis=1, keepdims=True)
    before = top[te]
    now = jnp.maximum(before, peak)
    acc[te] = acc[te] * jnp.exp2(before - now) + total * jnp.exp2(peak - now)
    top[te] = now


def columns(acc, top, cols):
    lane = lax.broadcasted_iota(jnp.int32, (CS, HALF), 1)
    batch = 1 if top is not None else 8

    def some(i, packed):
        for j in range(batch):
            te = i * batch + j
            if top is not None:
                value = jnp.max(top[te] + jnp.log(acc[te]) * LOG2E, axis=1, keepdims=True)
            else:
                value = jnp.sum(acc[te], axis=1, keepdims=True)
            packed = jnp.where(lane == te, value, packed)
        return packed

    packed = lax.fori_loop(0, 3 * CL // batch, some, jnp.zeros((CS, HALF), F32))
    for h in range(2):
        turned = jnp.transpose(packed[h * HALF : (h + 1) * HALF, :])
        for t in range(3):
            cols[pl.ds(t * 2 * CL + h, CL, stride=2), :] = turned[t * CL : (t + 1) * CL, :]


def in_range(*values):
    lowest = functools.reduce(jnp.minimum, [jnp.min(value) for value in values])
    highest = functools.reduce(jnp.maximum, [jnp.max(value) for value in values])
    return jnp.logical_and(lowest > TINY, highest < HUGE)


def build_left2(left, bias_g, bias, left2):
    row8 = lax.broadcasted_iota(jnp.int32, (8, HALF), 0)
    ones = jnp.where(row8 < 3, 1.0, 0.0)
    for t in range(3):
        for h in range(2):
            if t == 0:
                value = bias_g[pl.ds(h, CL, stride=2), :]
            else:
                value = bias[pl.ds(t * SPAN + h, CL, stride=2), :]
            high, middle, low = split3(value)
            stack = jnp.concatenate(
                [jnp.zeros((D, HALF), F32), high, middle, low, ones, jnp.zeros((32, HALF), F32)], axis=0
            )
            turned = jnp.transpose(stack).astype(BF16)
            for e in range(CL):
                cluster = e if t == 1 else CL + e
                here = pl.ds(h * HALF, HALF)
                left2[t * CL + e, here, :] = left[cluster, here, pl.ds(HALF, HALF)] + turned


def local_kernel(left, right, bias_g, bias, left2, log_cols, log_own, acc, top, own):
    span = SPAN
    build_left2(left, bias_g, bias, left2)

    def sweep(finish):
        for t in range(3):

            def some(i, _):
                for j in range(LOCAL_GROUP):
                    e = i * LOCAL_GROUP + j
                    at = t * span + 2 * e
                    a = jnp.concatenate([bias[pl.ds(at, 1), :], bias[pl.ds(at + 1, 1), :]], axis=1)
                    source = CL + e if t == 2 else e
                    z = scores(
                        left[e if t == 1 else CL + e, :, 0:HALF], left2[t * CL + e],
                        right[source, 0:D, :], right[source, D:HALF, :], a, e,
                    )
                    finish(z, a, t, e)
                return 0

            lax.fori_loop(0, CL // LOCAL_GROUP, some, 0)

    def fast(z, a, t, e):
        value = jnp.exp2(z)
        if t == 0:
            put_row(own, 2 * e, row_sum(value, a))
        acc[t * CL + e] = fold(value)

    def slow(z, a, t, e):
        if t == 0:
            put_row(own, 2 * e, row_log_sum(z))
        merge_columns(z, t * CL + e, acc, top)

    sweep(fast)
    columns(acc, None, log_cols)
    real = jnp.concatenate([bias_g[...], bias[span : 3 * span, :]], axis=0) > REAL
    cols = jnp.where(real, log_cols[...], 1.0)
    within = in_range(own[...], cols)

    @pl.when(within)
    def _():
        log_own[...] = jnp.log(own[...]) * LOG2E
        log_cols[...] = jnp.log(cols) * LOG2E

    @pl.when(jnp.logical_not(within))
    def _():
        acc[...] = jnp.zeros_like(acc)
        top[...] = jnp.full_like(top, 3.0 * NEGATIVE)
        sweep(slow)
        columns(acc, top, log_cols)
        log_own[...] = own[...]


def local_tiles(left, right, bias_g, bias):
    vmem = pl.BlockSpec(memory_space=pltpu.VMEM)
    return pl.pallas_call(
        local_kernel,
        out_shape=(
            jax.ShapeDtypeStruct((3 * CL, CS, HALF), BF16),
            jax.ShapeDtypeStruct((6 * CL, HALF), F32),
            jax.ShapeDtypeStruct((2 * CL, HALF), F32),
        ),
        in_specs=[vmem] * 4,
        out_specs=(vmem,) * 3,
        scratch_shapes=[
            pltpu.VMEM((3 * CL, CS, HALF), F32),
            pltpu.VMEM((3 * CL, CS, HALF), F32),
            pltpu.VMEM((2 * CL, HALF), F32),
        ],
        name="local_tiles",
    )(left, right, bias_g, bias)


def fetch_all(moved, held, sems):
    step = moved.shape[0] // PIECES

    def fetch(i):
        part = pl.ds(i * step, step)
        return pltpu.make_async_copy(moved.at[part], held.at[part], sems.at[i])

    for i in range(PIECES):
        fetch(i).start()
    return fetch


class Tiles:
    def __init__(self, held, left, slots, targets, bounds):
        self.held, self.left = held, left
        self.slots, self.targets, self.bounds = slots, targets, bounds
        self.devices = held.shape[0]
        self.live = bounds[self.devices - 1]

    def run(self, size, left2, inbox, finish):
        held, left = self.held, self.left

        def body(i, _):
            for j in range(size):
                n = i * size + j
                s, te = self.slots[n], self.targets[n]
                e = te % CL
                cluster = jnp.where(te // CL == 1, e, CL + e)
                spot = jnp.where(n < self.live, s, self.devices)
                high, low = split2(jnp.concatenate([held[s, 0:D, :], held[s, D : 2 * D, :]], axis=1))
                if inbox is None:
                    pair = held[s, 2 * D : 2 * D + 1, :], held[s, 2 * D + 1 : 2 * D + 2, :]
                else:
                    pair = inbox[pl.ds(4 * s + 2, 1), :], inbox[pl.ds(4 * s + 3, 1), :]
                a = jnp.where(n < self.live, jnp.concatenate(pair, axis=1), LOG2E * NEGATIVE)
                z = scores(left[cluster, :, 0:HALF], left2[te], high, low, a, e)
                finish(z, a, te, spot)
            return 0

        return body

    def sweep(self, left2, inbox, finish, fetch=None):
        run = self.run(GROUP, left2, inbox, finish)
        groups = (self.live + GROUP - 1) // GROUP
        if fetch is None:
            lax.fori_loop(0, groups, run, 0)
            return
        step = self.devices // PIECES

        def piece(i, start):
            fetch(i).wait()
            ready = self.bounds[(i + 1) * step - 1]
            stop = jnp.where(i == PIECES - 1, groups, ready // GROUP)
            lax.fori_loop(start, stop, run, 0)
            return stop

        lax.fori_loop(0, PIECES, piece, 0)

    def slow_sweep(self, left2, inbox, finish):
        lax.fori_loop(0, self.live, self.run(1, left2, inbox, finish), 0)


def column_pass(tiles, left2, inbox, fetch, acc, top, cols, start_g, start, named, sums=None):
    def fast(z, a, te, spot):
        value = jnp.exp2(z)
        if sums is not None:
            put_row(sums, 2 * spot, row_sum(value, a))
        acc[te] = acc[te] + fold(value)

    def slow(z, a, te, spot):
        if sums is not None:
            put_row(sums, 2 * spot, row_log_sum(z))
        merge_columns(z, te, acc, top)

    tiles.sweep(left2, inbox, fast, fetch)
    columns(acc, None, cols)
    real = jnp.concatenate([start_g[...], start[SPAN : 3 * SPAN, :]], axis=0) > REAL
    linear = jnp.where(jnp.logical_and(real, named), cols[...], 1.0)
    within = in_range(linear) if sums is None else in_range(sums[...], linear)

    @pl.when(within)
    def _():
        cols[...] = jnp.where(named, jnp.log(linear) * LOG2E, NEGATIVE)

    @pl.when(jnp.logical_not(within))
    def _():
        acc[...] = jnp.zeros_like(acc)
        top[...] = jnp.full_like(top, 3.0 * NEGATIVE)
        tiles.slow_sweep(left2, inbox, slow)
        columns(acc, top, cols)
        cols[...] = jnp.where(named, cols[...], NEGATIVE)

    return within


def first_kernel(
    moved, left, left2, start_g, start, back, log_cols, slots, targets, bounds, listed,
    held, acc, top, sums, codes, count, sems,
):
    devices = moved.shape[0]
    tags = pltpu.make_async_copy(moved.at[:, pl.ds(2 * D + 2, 1), :], codes, sems.at[PIECES])
    tags.start()
    fetch = fetch_all(moved, held, sems)
    acc[...] = jnp.zeros_like(acc)
    sums[...] = jnp.ones_like(sums)
    for te in range(3 * CL):
        count[te] = 0
    tags.wait()

    def gather(s, n):
        code = codes[s, 0, 0].astype(jnp.int32)

        @pl.when(code > 0)
        def _():
            slots[n] = s
            targets[n] = code - 1
            count[code - 1] = 1

        n = n + (code > 0).astype(jnp.int32)
        bounds[s] = n
        return n

    live = lax.fori_loop(0, devices, gather, 0, unroll=8)
    row = lax.broadcasted_iota(jnp.int32, listed.shape, 0) // 2
    some_listed = jnp.zeros(listed.shape, jnp.int32)
    for te in range(3 * CL):
        some_listed = jnp.where(row == te, count[te], some_listed)
    listed[...] = some_listed
    for i in range(GROUP):
        slots[live + i] = slots[0]
        targets[live + i] = 0
    tiles = Tiles(held, left, slots, targets, bounds)
    named = some_listed > 0
    within = column_pass(tiles, left2, None, fetch, acc, top, log_cols, start_g, start, named, sums)

    @pl.when(within)
    def _():
        back[...] = jnp.log(sums[0 : 2 * devices, :]) * LOG2E

    @pl.when(jnp.logical_not(within))
    def _():
        back[...] = sums[0 : 2 * devices, :]


SMEM = pl.BlockSpec(memory_space=pltpu.SMEM)
VMEM = pl.BlockSpec(memory_space=pltpu.VMEM)
HBM = pl.BlockSpec(memory_space=pl.ANY)


def shape(*dims, dtype=F32):
    return jax.ShapeDtypeStruct(dims, dtype)


def first_tiles(moved, left, left2, start_g, start):
    devices = moved.shape[0]
    out = pl.pallas_call(
        first_kernel,
        out_shape=(
            shape(2 * devices, HALF),
            shape(3 * SPAN, HALF),
            shape(devices + GROUP, dtype=jnp.int32),
            shape(devices + GROUP, dtype=jnp.int32),
            shape(devices, dtype=jnp.int32),
            shape(3 * SPAN, HALF, dtype=jnp.int32),
        ),
        in_specs=[HBM] + [VMEM] * 4,
        out_specs=(VMEM, VMEM, SMEM, SMEM, SMEM, VMEM),
        scratch_shapes=[
            pltpu.VMEM((devices, ROWS, HALF), F32),
            pltpu.VMEM((3 * CL, CS, HALF), F32),
            pltpu.VMEM((3 * CL, CS, HALF), F32),
            pltpu.VMEM((2 * devices + 8, HALF), F32),
            pltpu.SMEM((devices, 1, HALF), F32),
            pltpu.SMEM((3 * CL,), jnp.int32),
            pltpu.SemaphoreType.DMA((PIECES + 1,)),
        ],
        name="first_tiles",
    )(moved, left, left2, start_g, start)
    return out[0], out[1], out[2:5], out[5]


def log_sum(values):
    peak = functools.reduce(jnp.maximum, values)
    total = functools.reduce(jnp.add, [jnp.exp2(value - peak) for value in values])
    return peak + jnp.log(total) * LOG2E


def fresh(total, weight, half, potential):
    value = 0.5 * (potential - DAMPING * EPSILON * (LN2 * total - half / EPSILON))
    return jnp.where(weight > REAL, value, 0.0)


def update_g_kernel(cols_local, cols_moved, weight, half, start_g, new, new_bias):
    side, span = slice(SPAN, 2 * SPAN), slice(0, SPAN)
    total = log_sum([cols_local[span, :], cols_moved[span, :]]) - start_g[...]
    value = fresh(total, weight[side, :], half[side, :], 0.0)
    new[...] = value
    new_bias[...] = bias_of(weight[side, :], half[side, :], value)


def update_g(*args):
    return pl.pallas_call(
        update_g_kernel,
        out_shape=(shape(SPAN, HALF),) * 2,
        in_specs=[VMEM] * 5,
        out_specs=(VMEM,) * 2,
        name="update_g",
    )(*args)


def step_kernel(has_columns, has_rows, *refs):
    refs = list(refs)
    take = lambda n: [refs.pop(0) for _ in range(n)]
    cross, xself, yself, slots, targets, bounds, moved = take(7)
    inbox, cols_local, log_own, cols_moved, weight, half, start_g, start, left = take(9)
    if has_columns:
        listed = cols_moved
        bias_g, bias, potential_g, potential, left2_start = take(5)
    else:
        bias = start
        (new_bias_g,) = take(1)
    if not has_rows:
        new_f, new_g, new_p, new_q = take(4)
    else:
        new_g, new_bias_g = take(2) if has_columns else (None, new_bias_g)
        new, new_bias, outbox = take(3)
    held, parts, sems = take(3)
    if has_columns:
        acc, top, cols_moved = take(3)
    if has_rows:
        left2, sums = take(2)
    devices = moved.shape[0]
    fetch = fetch_all(moved, held, sems)
    counts = (cross.shape[1], xself.shape[0], yself.shape[0])
    offsets = (0, counts[0], counts[0] + counts[1])
    requests = list(lists(cross, xself, yself))
    width = inbox.shape[0] // devices
    for kind, c, k, wanted in requests:
        at = pl.multiple_of(width * (wanted // CL), width)
        parts[offsets[kind] + k, 2 * c : 2 * c + 2, :] = inbox[pl.ds(at, 2), :]
    if has_rows:
        sums[...] = jnp.ones_like(sums)
    tiles = Tiles(held, left, slots, targets, bounds)
    if has_columns:
        acc[...] = jnp.zeros_like(acc)
        column_pass(
            tiles, left2_start, inbox, fetch, acc, top, cols_moved, start_g, start, listed[...] > 0
        )
    f, p, q = (slice(i * SPAN, (i + 1) * SPAN) for i in range(3))
    answers = [
        [parts[offsets[t] + k] - start[t * SPAN : (t + 1) * SPAN, :] for k in range(counts[t])]
        for t in range(3)
    ]
    totals = [log_sum([log_own[...] - bias[f, :]] + answers[0])]
    for here, answer in ((p, answers[1]), (q, answers[2])):
        totals.append(
            log_sum([cols_local[here, :] - bias[here, :], cols_moved[here, :] - start[here, :]] + answer)
        )
    for i, total in enumerate(totals):
        here = (f, p, q)[i]
        side = slice(SPAN, 2 * SPAN) if i == 2 else slice(0, SPAN)
        before = potential[here, :] if has_columns else 0.0
        value = fresh(total, weight[side, :], half[side, :], before)
        if has_rows:
            new[here, :] = value
            new_bias[here, :] = bias_of(weight[side, :], half[side, :], value)
        else:
            (new_f, new_p, new_q)[i][...] = value
    if has_columns:
        side = slice(SPAN, 2 * SPAN)
        total = log_sum([cols_local[f, :] - bias_g[...], cols_moved[f, :] - start_g[...]])
        value = fresh(total, weight[side, :], half[side, :], potential_g[...])
        new_g[...] = value
        if has_rows:
            new_bias_g[...] = bias_of(weight[side, :], half[side, :], value)
    if not has_rows:
        return
    for kind, c, _, wanted in requests:
        at = pl.multiple_of(4 * (wanted // CL) + 2, 2)
        base = kind * SPAN + 2 * c
        outbox[pl.ds(at, 2), :] = new_bias[base : base + 2, :]
    build_left2(left, new_bias_g, new_bias, left2)

    def fast(z, a, te, spot):
        put_row(sums, 4 * spot, row_sum(jnp.exp2(z), a))

    def slow(z, a, te, spot):
        put_row(sums, 4 * spot, row_log_sum(z))

    tiles.sweep(left2, None, fast, None if has_columns else fetch)
    within = in_range(sums[...])
    answer_row = lax.broadcasted_iota(jnp.int32, outbox.shape, 0) % 4 < 2

    @pl.when(within)
    def _():
        outbox[...] = jnp.where(answer_row, jnp.log(sums[0 : 4 * devices, :]) * LOG2E, outbox[...])

    @pl.when(jnp.logical_not(within))
    def _():
        tiles.slow_sweep(left2, None, slow)
        outbox[...] = jnp.where(answer_row, sums[0 : 4 * devices, :], outbox[...])


def step(has_columns, has_rows, tables, index, moved, *args):
    devices = moved.shape[0]
    listed = tables[0].shape[1] + tables[1].shape[0] + tables[2].shape[0]
    one, three = shape(SPAN, HALF), shape(3 * SPAN, HALF)
    if has_rows:
        outs = ([one, one] if has_columns else []) + [three, three, shape(4 * devices, HALF)]
    else:
        outs = [one] * 4
    scratch = [
        pltpu.VMEM((devices, ROWS, HALF), F32),
        pltpu.VMEM((listed, SPAN, HALF), F32),
        pltpu.SemaphoreType.DMA((PIECES,)),
    ]
    if has_columns:
        scratch += [pltpu.VMEM((3 * CL, CS, HALF), F32)] * 2 + [pltpu.VMEM((3 * SPAN, HALF), F32)]
    if has_rows:
        scratch += [pltpu.VMEM((3 * CL, CS, HALF), BF16), pltpu.VMEM((4 * devices + 8, HALF), F32)]
    return pl.pallas_call(
        functools.partial(step_kernel, has_columns, has_rows),
        out_shape=outs,
        in_specs=[SMEM] * 6 + [HBM] + [VMEM] * len(args),
        out_specs=[VMEM] * len(outs),
        scratch_shapes=scratch,
        name="step_" + "c" * has_columns + "r" * has_rows,
    )(*tables, *index, moved, *args)


def exchange(blocks):
    return lax.all_to_all(blocks, AXES, split_axis=0, concat_axis=0, tiled=True)


def exchange_rows(rows, devices):
    wide = rows.reshape(devices, rows.shape[0] // devices, HALF)
    return exchange(wide).reshape(rows.shape)


def local(x, y, x_logmass, y_logmass, x_sizes, y_sizes, cross, xself, yself):
    devices = lax.axis_size(AXES)
    tables = (cross, xself.T, yself.T)
    send, weight, half, start_g, start = push(
        *tables, x_sizes, y_sizes, x, y,
        x_logmass.reshape(SPAN, HALF), y_logmass.reshape(SPAN, HALF), devices,
    )
    moved = exchange(send)
    left, right = left_side(x, y)
    left2, cols_local, log_own = local_tiles(left, right, start_g, start)
    back, cols_moved, index, listed = first_tiles(moved, left, left2, start_g, start)
    inbox = exchange_rows(back, devices)
    potential_g, bias_g = update_g(cols_local, cols_moved, weight, half, start_g)
    potential, bias, outbox = step(
        False, True, tables, index, moved,
        inbox, cols_local, log_own, cols_moved, weight, half, start_g, start, left, bias_g,
    )
    for iteration in range(1, ITERS):
        last = iteration == ITERS - 1
        inbox = exchange_rows(outbox, devices)
        _, cols_local, log_own = local_tiles(left, right, bias_g, bias)
        out = step(
            True, not last, tables, index, moved,
            inbox, cols_local, log_own, listed, weight, half, start_g, start, left,
            bias_g, bias, potential_g, potential, left2,
        )
        if not last:
            potential_g, bias_g, potential, bias, outbox = out
    return tuple(part.reshape(SPAN * HALF) for part in out)


def solution(mesh):
    flat, table = P(AXES), P(AXES, None)
    points = P(None, AXES)
    return jax.shard_map(
        local,
        mesh=mesh,
        in_specs=(points, points, flat, flat, table, table, table, table, table),
        out_specs=(flat, flat, flat, flat),
        check_vma=False,
    )
```

```python
import functools

import jax
import jax.numpy as jnp
from jax import lax
from jax.experimental import pallas as pl
from jax.experimental.pallas import tpu as pltpu
from jax.sharding import PartitionSpec as P

ITERS = 3
EPSILON = 0.5
DAMPING = 2.0 / (2.0 + 0.5)
NEGATIVE = -1e30
REAL = -1e29
LOG2E = 1.4426950408889634
LN2 = 0.6931471805599453
TINY = 2.0**-90
HUGE = 2.0**90
AXES = ("row", "col")

D = 64
CS = 256
CL = 8
HALF = 128
ROWS = 2 * D + 8
GROUP = 8
LOCAL_GROUP = 4
PIECES = 8
SPAN = 16
BF16 = jnp.bfloat16
F32 = jnp.float32


def lists(cross, xself, yself):
    for c in range(cross.shape[0]):
        for k in range(cross.shape[1]):
            yield 0, c, k, cross[c, k]
    for table, kind in ((xself, 1), (yself, 2)):
        for c in range(table.shape[1]):
            for k in range(table.shape[0]):
                yield kind, c, k, table[k, c]


def bias_of(weight, half, potential):
    return LOG2E * (weight + (potential - half) / EPSILON)


def push_kernel(
    cross, xself, yself, x_sizes, y_sizes, x_ref, y_ref, x_mass, y_mass,
    send, weight_ref, half_ref, bias_g_ref, bias_ref, aux, sems,
):
    devices = send.shape[0]
    requests = list(lists(cross, xself, yself))
    for kind, c, _, named in requests:
        owner = named // CL
        source = y_ref if kind == 2 else x_ref
        for h in range(2):
            pltpu.make_async_copy(
                source.at[:, pl.ds(c * CS + h * HALF, HALF)],
                send.at[owner, pl.ds(h * D, D), :],
                sems.at[0],
            ).start()
    row = lax.broadcasted_iota(jnp.int32, (2 * CL, HALF), 0)
    position = (row % 2) * HALF + lax.broadcasted_iota(jnp.int32, (2 * CL, HALF), 1)
    for side, (points, sizes, mass) in enumerate(
        ((x_ref, x_sizes, x_mass), (y_ref, y_sizes, y_mass))
    ):
        count = jnp.zeros((2 * CL, HALF), jnp.int32)
        for c in range(CL):
            count = jnp.where(row // 2 == c, sizes[0, c], count)
        base = side * 2 * CL
        weight_ref[base : base + 2 * CL, :] = jnp.where(position < count, mass[...], NEGATIVE)
        for t in range(2 * CL):
            piece = points[:, t * HALF : (t + 1) * HALF]
            half_ref[base + t : base + t + 1, :] = 0.5 * jnp.sum(piece * piece, axis=0, keepdims=True)
    bias = bias_of(weight_ref[...], half_ref[...], 0.0)
    bias_ref[0 : 2 * CL, :] = bias[0 : 2 * CL, :]
    bias_ref[2 * CL : 6 * CL, :] = bias
    bias_g_ref[...] = bias[2 * CL : 4 * CL, :]
    aux[...] = jnp.zeros_like(aux)
    for kind, c, _, named in requests:
        owner = named // CL
        base = kind * 2 * CL + 2 * c
        aux[owner, 0:2, :] = bias_ref[base : base + 2, :]
        code = (kind * CL + named % CL + 1).astype(F32)
        aux[owner, 2:3, :] = jnp.full((1, HALF), code, F32)
    tail = pltpu.make_async_copy(aux, send.at[:, pl.ds(2 * D, 8), :], sems.at[1])
    tail.start()
    tail.wait()
    sent = send.at[pl.ds(0, len(requests)), pl.ds(0, 2 * D), :]
    pltpu.make_async_copy(sent, sent, sems.at[0]).wait()


def push(cross, xself, yself, x_sizes, y_sizes, x, y, x_mass, y_mass, devices):
    smem = pl.BlockSpec(memory_space=pltpu.SMEM)
    vmem = pl.BlockSpec(memory_space=pltpu.VMEM)
    return pl.pallas_call(
        push_kernel,
        out_shape=(
            jax.ShapeDtypeStruct((devices, ROWS, HALF), F32),
            jax.ShapeDtypeStruct((4 * CL, HALF), F32),
            jax.ShapeDtypeStruct((4 * CL, HALF), F32),
            jax.ShapeDtypeStruct((2 * CL, HALF), F32),
            jax.ShapeDtypeStruct((6 * CL, HALF), F32),
        ),
        in_specs=[smem] * 5 + [vmem] * 4,
        out_specs=(pl.BlockSpec(memory_space=pl.ANY), vmem, vmem, vmem, vmem),
        scratch_shapes=[
            pltpu.VMEM((devices, 8, HALF), F32),
            pltpu.SemaphoreType.DMA((2,)),
        ],
        name="push",
    )(cross, xself, yself, x_sizes, y_sizes, x, y, x_mass, y_mass)


def split2(value):
    high = value.astype(BF16)
    return high, (value - high.astype(F32)).astype(BF16)


def split3(value):
    high = value.astype(BF16).astype(F32)
    rest = value - high
    middle = rest.astype(BF16).astype(F32)
    return high, middle, rest - middle


def left_kernel(x_ref, y_ref, left_ref, right_ref):
    lane = lax.broadcasted_iota(jnp.int32, (CS, HALF), 1)
    for side, points in enumerate((x_ref, y_ref)):
        for c in range(CL):
            piece = points[:, c * CS : (c + 1) * CS]
            scaled = piece * (LOG2E / EPSILON)
            turned = jnp.transpose(jnp.concatenate([scaled, scaled], axis=0))
            high, low = split2(turned)
            left_ref[side * CL + c, :, 0:HALF] = high
            low = jnp.where(lane < D, low.astype(F32), 0.0)
            left_ref[side * CL + c, :, HALF:CS] = low.astype(BF16)
            high, low = split2(piece)
            right_ref[side * CL + c, 0:D, :] = high
            right_ref[side * CL + c, D:HALF, :] = low


def left_side(x, y):
    vmem = pl.BlockSpec(memory_space=pltpu.VMEM)
    return pl.pallas_call(
        left_kernel,
        out_shape=(
            jax.ShapeDtypeStruct((2 * CL, CS, CS), BF16),
            jax.ShapeDtypeStruct((2 * CL, HALF, CS), BF16),
        ),
        in_specs=[vmem, vmem],
        out_specs=(vmem, vmem),
        name="left_side",
    )(x, y)


def scores(left_high, left_rest, high, low, a, e):
    a1, a2, a3 = split3(a)
    row = lax.broadcasted_iota(jnp.int32, (8, CS), 0)
    pick = jnp.where(row == e, 1.0, 0.0)
    mine = jnp.where(row == 0, a1, jnp.where(row == 1, a2, jnp.where(row == 2, a3, 0.0)))
    tail = jnp.concatenate([pick, pick, pick, mine], axis=0).astype(BF16)
    right = jnp.concatenate([high, low, high, tail, jnp.zeros((32, CS), BF16)], axis=0)
    return jnp.dot(
        jnp.concatenate([left_high, left_rest], axis=1), right, preferred_element_type=F32
    )


def put_row(out, at, value):
    out[pl.ds(at, 1), :] = value[:, 0:HALF]
    out[pl.ds(at + 1, 1), :] = value[:, HALF:CS]


def row_sum(value, a):
    return jnp.where(a > REAL, jnp.sum(value, axis=0, keepdims=True), 1.0)


def fold(value):
    return value[:, 0:HALF] + value[:, HALF:CS]


def row_log_sum(z):
    peak = jnp.max(z, axis=0, keepdims=True)
    total = jnp.sum(jnp.exp2(z - peak), axis=0, keepdims=True)
    return peak + jnp.log(total) * LOG2E


def merge_columns(z, te, acc, top):
    peak = jnp.max(z, axis=1, keepdims=True)
    total = jnp.sum(jnp.exp2(z - peak), axis=1, keepdims=True)
    before = top[te]
    now = jnp.maximum(before, peak)
    acc[te] = acc[te] * jnp.exp2(before - now) + total * jnp.exp2(peak - now)
    top[te] = now


def columns(acc, top, cols):
    lane = lax.broadcasted_iota(jnp.int32, (CS, HALF), 1)
    batch = 1 if top is not None else 8

    def some(i, packed):
        for j in range(batch):
            te = i * batch + j
            if top is not None:
                value = jnp.max(top[te] + jnp.log(acc[te]) * LOG2E, axis=1, keepdims=True)
            else:
                value = jnp.sum(acc[te], axis=1, keepdims=True)
            packed = jnp.where(lane == te, value, packed)
        return packed

    packed = lax.fori_loop(0, 3 * CL // batch, some, jnp.zeros((CS, HALF), F32))
    for h in range(2):
        turned = jnp.transpose(packed[h * HALF : (h + 1) * HALF, :])
        for t in range(3):
            cols[pl.ds(t * 2 * CL + h, CL, stride=2), :] = turned[t * CL : (t + 1) * CL, :]


def in_range(*values):
    lowest = functools.reduce(jnp.minimum, [jnp.min(value) for value in values])
    highest = functools.reduce(jnp.maximum, [jnp.max(value) for value in values])
    return jnp.logical_and(lowest > TINY, highest < HUGE)


def build_left2(left, bias_g, bias, left2):
    row8 = lax.broadcasted_iota(jnp.int32, (8, HALF), 0)
    ones = jnp.where(row8 < 3, 1.0, 0.0)
    for t in range(3):
        for h in range(2):
            if t == 0:
                value = bias_g[pl.ds(h, CL, stride=2), :]
            else:
                value = bias[pl.ds(t * SPAN + h, CL, stride=2), :]
            high, middle, low = split3(value)
            stack = jnp.concatenate(
                [jnp.zeros((D, HALF), F32), high, middle, low, ones, jnp.zeros((32, HALF), F32)], axis=0
            )
            turned = jnp.transpose(stack).astype(BF16)
            for e in range(CL):
                cluster = e if t == 1 else CL + e
                here = pl.ds(h * HALF, HALF)
                left2[t * CL + e, here, :] = left[cluster, here, pl.ds(HALF, HALF)] + turned


def local_kernel(left, right, bias_g, bias, left2, log_cols, log_own, acc, top, own):
    span = SPAN
    build_left2(left, bias_g, bias, left2)

    def sweep(finish):
        for t in range(3):

            def some(i, _):
                for j in range(LOCAL_GROUP):
                    e = i * LOCAL_GROUP + j
                    at = t * span + 2 * e
                    a = jnp.concatenate([bias[pl.ds(at, 1), :], bias[pl.ds(at + 1, 1), :]], axis=1)
                    source = CL + e if t == 2 else e
                    z = scores(
                        left[e if t == 1 else CL + e, :, 0:HALF], left2[t * CL + e],
                        right[source, 0:D, :], right[source, D:HALF, :], a, e,
                    )
                    finish(z, a, t, e)
                return 0

            lax.fori_loop(0, CL // LOCAL_GROUP, some, 0)

    def fast(z, a, t, e):
        value = jnp.exp2(z)
        if t == 0:
            put_row(own, 2 * e, row_sum(value, a))
        acc[t * CL + e] = fold(value)

    def slow(z, a, t, e):
        if t == 0:
            put_row(own, 2 * e, row_log_sum(z))
        merge_columns(z, t * CL + e, acc, top)

    sweep(fast)
    columns(acc, None, log_cols)
    real = jnp.concatenate([bias_g[...], bias[span : 3 * span, :]], axis=0) > REAL
    cols = jnp.where(real, log_cols[...], 1.0)
    within = in_range(own[...], cols)

    @pl.when(within)
    def _():
        log_own[...] = jnp.log(own[...]) * LOG2E
        log_cols[...] = jnp.log(cols) * LOG2E

    @pl.when(jnp.logical_not(within))
    def _():
        acc[...] = jnp.zeros_like(acc)
        top[...] = jnp.full_like(top, 3.0 * NEGATIVE)
        sweep(slow)
        columns(acc, top, log_cols)
        log_own[...] = own[...]


def local_tiles(left, right, bias_g, bias):
    vmem = pl.BlockSpec(memory_space=pltpu.VMEM)
    return pl.pallas_call(
        local_kernel,
        out_shape=(
            jax.ShapeDtypeStruct((3 * CL, CS, HALF), BF16),
            jax.ShapeDtypeStruct((6 * CL, HALF), F32),
            jax.ShapeDtypeStruct((2 * CL, HALF), F32),
        ),
        in_specs=[vmem] * 4,
        out_specs=(vmem,) * 3,
        scratch_shapes=[
            pltpu.VMEM((3 * CL, CS, HALF), F32),
            pltpu.VMEM((3 * CL, CS, HALF), F32),
            pltpu.VMEM((2 * CL, HALF), F32),
        ],
        name="local_tiles",
    )(left, right, bias_g, bias)


def fetch_all(moved, held, sems):
    step = moved.shape[0] // PIECES

    def fetch(i):
        part = pl.ds(i * step, step)
        return pltpu.make_async_copy(moved.at[part], held.at[part], sems.at[i])

    for i in range(PIECES):
        fetch(i).start()
    return fetch


def bring(pairs, sems, base):
    copies = [pltpu.make_async_copy(a, b, sems.at[base + i]) for i, (a, b) in enumerate(pairs)]
    for copy in copies:
        copy.start()
    return copies


class Tiles:
    def __init__(self, held, left, slots, targets, bounds):
        self.held, self.left = held, left
        self.slots, self.targets, self.bounds = slots, targets, bounds
        self.devices = held.shape[0]
        self.live = bounds[self.devices - 1]

    def run(self, size, left2, inbox, finish):
        held, left = self.held, self.left

        def body(i, _):
            for j in range(size):
                n = i * size + j
                s, te = self.slots[n], self.targets[n]
                e = te % CL
                cluster = jnp.where(te // CL == 1, e, CL + e)
                spot = jnp.where(n < self.live, s, self.devices)
                high, low = split2(jnp.concatenate([held[s, 0:D, :], held[s, D : 2 * D, :]], axis=1))
                if inbox is None:
                    pair = held[s, 2 * D : 2 * D + 1, :], held[s, 2 * D + 1 : 2 * D + 2, :]
                else:
                    pair = inbox[pl.ds(4 * s + 2, 1), :], inbox[pl.ds(4 * s + 3, 1), :]
                a = jnp.where(n < self.live, jnp.concatenate(pair, axis=1), LOG2E * NEGATIVE)
                z = scores(left[cluster, :, 0:HALF], left2[te], high, low, a, e)
                finish(z, a, te, spot)
            return 0

        return body

    def sweep(self, left2, inbox, finish, fetch=None):
        run = self.run(GROUP, left2, inbox, finish)
        groups = (self.live + GROUP - 1) // GROUP
        if fetch is None:
            lax.fori_loop(0, groups, run, 0)
            return
        step = self.devices // PIECES

        def piece(i, start):
            fetch(i).wait()
            ready = self.bounds[(i + 1) * step - 1]
            stop = jnp.where(i == PIECES - 1, groups, ready // GROUP)
            lax.fori_loop(start, stop, run, 0)
            return stop

        lax.fori_loop(0, PIECES, piece, 0)

    def slow_sweep(self, left2, inbox, finish):
        lax.fori_loop(0, self.live, self.run(1, left2, inbox, finish), 0)


def column_pass(tiles, left2, inbox, fetch, acc, top, cols, start_g, start, named, sums=None):
    def fast(z, a, te, spot):
        value = jnp.exp2(z)
        if sums is not None:
            put_row(sums, 2 * spot, row_sum(value, a))
        acc[te] = acc[te] + fold(value)

    def slow(z, a, te, spot):
        if sums is not None:
            put_row(sums, 2 * spot, row_log_sum(z))
        merge_columns(z, te, acc, top)

    tiles.sweep(left2, inbox, fast, fetch)
    columns(acc, None, cols)
    real = jnp.concatenate([start_g[...], start[SPAN : 3 * SPAN, :]], axis=0) > REAL
    linear = jnp.where(jnp.logical_and(real, named), cols[...], 1.0)
    within = in_range(linear) if sums is None else in_range(sums[...], linear)

    @pl.when(within)
    def _():
        cols[...] = jnp.where(named, jnp.log(linear) * LOG2E, NEGATIVE)

    @pl.when(jnp.logical_not(within))
    def _():
        acc[...] = jnp.zeros_like(acc)
        top[...] = jnp.full_like(top, 3.0 * NEGATIVE)
        tiles.slow_sweep(left2, inbox, slow)
        columns(acc, top, cols)
        cols[...] = jnp.where(named, cols[...], NEGATIVE)

    return within


def first_kernel(
    moved, left_hbm, left2_hbm, start_g, start, back, log_cols, slots, targets, bounds, listed,
    held, acc, top, sums, codes, count, sems, left, left2,
):
    devices = moved.shape[0]
    tags = pltpu.make_async_copy(moved.at[:, pl.ds(2 * D + 2, 1), :], codes, sems.at[PIECES])
    tags.start()
    sides = bring(((left_hbm, left), (left2_hbm, left2)), sems, PIECES + 1)
    fetch = fetch_all(moved, held, sems)
    acc[...] = jnp.zeros_like(acc)
    sums[...] = jnp.ones_like(sums)
    for te in range(3 * CL):
        count[te] = 0
    tags.wait()

    def gather(s, n):
        code = codes[s, 0, 0].astype(jnp.int32)

        @pl.when(code > 0)
        def _():
            slots[n] = s
            targets[n] = code - 1
            count[code - 1] = 1

        n = n + (code > 0).astype(jnp.int32)
        bounds[s] = n
        return n

    live = lax.fori_loop(0, devices, gather, 0, unroll=8)
    row = lax.broadcasted_iota(jnp.int32, listed.shape, 0) // 2
    some_listed = jnp.zeros(listed.shape, jnp.int32)
    for te in range(3 * CL):
        some_listed = jnp.where(row == te, count[te], some_listed)
    listed[...] = some_listed
    for i in range(GROUP):
        slots[live + i] = slots[0]
        targets[live + i] = 0
    tiles = Tiles(held, left, slots, targets, bounds)
    named = some_listed > 0
    for copy in sides:
        copy.wait()
    within = column_pass(tiles, left2, None, fetch, acc, top, log_cols, start_g, start, named, sums)

    @pl.when(within)
    def _():
        back[...] = jnp.log(sums[0 : 2 * devices, :]) * LOG2E

    @pl.when(jnp.logical_not(within))
    def _():
        back[...] = sums[0 : 2 * devices, :]


SMEM = pl.BlockSpec(memory_space=pltpu.SMEM)
VMEM = pl.BlockSpec(memory_space=pltpu.VMEM)
HBM = pl.BlockSpec(memory_space=pl.ANY)


def shape(*dims, dtype=F32):
    return jax.ShapeDtypeStruct(dims, dtype)


def first_tiles(moved, left, left2, start_g, start):
    devices = moved.shape[0]
    out = pl.pallas_call(
        first_kernel,
        out_shape=(
            shape(2 * devices, HALF),
            shape(3 * SPAN, HALF),
            shape(devices + GROUP, dtype=jnp.int32),
            shape(devices + GROUP, dtype=jnp.int32),
            shape(devices, dtype=jnp.int32),
            shape(3 * SPAN, HALF, dtype=jnp.int32),
        ),
        in_specs=[HBM] * 3 + [VMEM] * 2,
        out_specs=(VMEM, VMEM, SMEM, SMEM, SMEM, VMEM),
        scratch_shapes=[
            pltpu.VMEM((devices, ROWS, HALF), F32),
            pltpu.VMEM((3 * CL, CS, HALF), F32),
            pltpu.VMEM((3 * CL, CS, HALF), F32),
            pltpu.VMEM((2 * devices + 8, HALF), F32),
            pltpu.SMEM((devices, 1, HALF), F32),
            pltpu.SMEM((3 * CL,), jnp.int32),
            pltpu.SemaphoreType.DMA((PIECES + 3,)),
            pltpu.VMEM((2 * CL, CS, CS), BF16),
            pltpu.VMEM((3 * CL, CS, HALF), BF16),
        ],
        name="first_tiles",
    )(moved, left, left2, start_g, start)
    return out[0], out[1], out[2:5], out[5]


def log_sum(values):
    peak = functools.reduce(jnp.maximum, values)
    total = functools.reduce(jnp.add, [jnp.exp2(value - peak) for value in values])
    return peak + jnp.log(total) * LOG2E


def fresh(total, weight, half, potential):
    value = 0.5 * (potential - DAMPING * EPSILON * (LN2 * total - half / EPSILON))
    return jnp.where(weight > REAL, value, 0.0)


def update_g_kernel(cols_local, cols_moved, weight, half, start_g, new, new_bias):
    side, span = slice(SPAN, 2 * SPAN), slice(0, SPAN)
    total = log_sum([cols_local[span, :], cols_moved[span, :]]) - start_g[...]
    value = fresh(total, weight[side, :], half[side, :], 0.0)
    new[...] = value
    new_bias[...] = bias_of(weight[side, :], half[side, :], value)


def update_g(*args):
    return pl.pallas_call(
        update_g_kernel,
        out_shape=(shape(SPAN, HALF),) * 2,
        in_specs=[VMEM] * 5,
        out_specs=(VMEM,) * 2,
        name="update_g",
    )(*args)


def step_kernel(has_columns, has_rows, *refs):
    refs = list(refs)
    take = lambda n: [refs.pop(0) for _ in range(n)]
    cross, xself, yself, slots, targets, bounds, moved = take(7)
    inbox, cols_local, log_own, cols_moved, weight, half, start_g, start = take(8)
    if has_columns:
        listed = cols_moved
        bias_g, bias, potential_g, potential, left_hbm, left2_hbm = take(6)
    else:
        bias = start
        new_bias_g, left_hbm = take(2)
    if not has_rows:
        new_f, new_g, new_p, new_q = take(4)
    else:
        new_g, new_bias_g = take(2) if has_columns else (None, new_bias_g)
        new, new_bias, outbox = take(3)
    held, parts, sems, left = take(4)
    if has_columns:
        acc, top, cols_moved, left2_start = take(4)
    if has_rows:
        left2, sums = take(2)
    devices = moved.shape[0]
    pairs = ((left_hbm, left), (left2_hbm, left2_start)) if has_columns else ((left_hbm, left),)
    sides = bring(pairs, sems, PIECES)
    fetch = fetch_all(moved, held, sems)
    counts = (cross.shape[1], xself.shape[0], yself.shape[0])
    offsets = (0, counts[0], counts[0] + counts[1])
    requests = list(lists(cross, xself, yself))
    width = inbox.shape[0] // devices
    for kind, c, k, wanted in requests:
        at = pl.multiple_of(width * (wanted // CL), width)
        parts[offsets[kind] + k, 2 * c : 2 * c + 2, :] = inbox[pl.ds(at, 2), :]
    if has_rows:
        sums[...] = jnp.ones_like(sums)
    tiles = Tiles(held, left, slots, targets, bounds)
    if has_columns:
        acc[...] = jnp.zeros_like(acc)
    for copy in sides:
        copy.wait()
    if has_columns:
        column_pass(
            tiles, left2_start, inbox, fetch, acc, top, cols_moved, start_g, start, listed[...] > 0
        )
    f, p, q = (slice(i * SPAN, (i + 1) * SPAN) for i in range(3))
    answers = [
        [parts[offsets[t] + k] - start[t * SPAN : (t + 1) * SPAN, :] for k in range(counts[t])]
        for t in range(3)
    ]
    totals = [log_sum([log_own[...] - bias[f, :]] + answers[0])]
    for here, answer in ((p, answers[1]), (q, answers[2])):
        totals.append(
            log_sum([cols_local[here, :] - bias[here, :], cols_moved[here, :] - start[here, :]] + answer)
        )
    for i, total in enumerate(totals):
        here = (f, p, q)[i]
        side = slice(SPAN, 2 * SPAN) if i == 2 else slice(0, SPAN)
        before = potential[here, :] if has_columns else 0.0
        value = fresh(total, weight[side, :], half[side, :], before)
        if has_rows:
            new[here, :] = value
            new_bias[here, :] = bias_of(weight[side, :], half[side, :], value)
        else:
            (new_f, new_p, new_q)[i][...] = value
    if has_columns:
        side = slice(SPAN, 2 * SPAN)
        total = log_sum([cols_local[f, :] - bias_g[...], cols_moved[f, :] - start_g[...]])
        value = fresh(total, weight[side, :], half[side, :], potential_g[...])
        new_g[...] = value
        if has_rows:
            new_bias_g[...] = bias_of(weight[side, :], half[side, :], value)
    if not has_rows:
        return
    for kind, c, _, wanted in requests:
        at = pl.multiple_of(4 * (wanted // CL) + 2, 2)
        base = kind * SPAN + 2 * c
        outbox[pl.ds(at, 2), :] = new_bias[base : base + 2, :]
    build_left2(left, new_bias_g, new_bias, left2)

    def fast(z, a, te, spot):
        put_row(sums, 4 * spot, row_sum(jnp.exp2(z), a))

    def slow(z, a, te, spot):
        put_row(sums, 4 * spot, row_log_sum(z))

    tiles.sweep(left2, None, fast, None if has_columns else fetch)
    within = in_range(sums[...])
    answer_row = lax.broadcasted_iota(jnp.int32, outbox.shape, 0) % 4 < 2

    @pl.when(within)
    def _():
        outbox[...] = jnp.where(answer_row, jnp.log(sums[0 : 4 * devices, :]) * LOG2E, outbox[...])

    @pl.when(jnp.logical_not(within))
    def _():
        tiles.slow_sweep(left2, None, slow)
        outbox[...] = jnp.where(answer_row, sums[0 : 4 * devices, :], outbox[...])


def step(has_columns, has_rows, tables, index, moved, *args):
    devices = moved.shape[0]
    listed = tables[0].shape[1] + tables[1].shape[0] + tables[2].shape[0]
    one, three = shape(SPAN, HALF), shape(3 * SPAN, HALF)
    sides = 2 if has_columns else 1
    if has_rows:
        outs = ([one, one] if has_columns else []) + [three, three, shape(4 * devices, HALF)]
    else:
        outs = [one] * 4
    scratch = [
        pltpu.VMEM((devices, ROWS, HALF), F32),
        pltpu.VMEM((listed, SPAN, HALF), F32),
        pltpu.SemaphoreType.DMA((PIECES + 2,)),
        pltpu.VMEM((2 * CL, CS, CS), BF16),
    ]
    if has_columns:
        scratch += [pltpu.VMEM((3 * CL, CS, HALF), F32)] * 2
        scratch += [pltpu.VMEM((3 * SPAN, HALF), F32), pltpu.VMEM((3 * CL, CS, HALF), BF16)]
    if has_rows:
        scratch += [pltpu.VMEM((3 * CL, CS, HALF), BF16), pltpu.VMEM((4 * devices + 8, HALF), F32)]
    return pl.pallas_call(
        functools.partial(step_kernel, has_columns, has_rows),
        out_shape=outs,
        in_specs=[SMEM] * 6 + [HBM] + [VMEM] * (len(args) - sides) + [HBM] * sides,
        out_specs=[VMEM] * len(outs),
        scratch_shapes=scratch,
        name="step_" + "c" * has_columns + "r" * has_rows,
    )(*tables, *index, moved, *args)


def exchange(blocks):
    return lax.all_to_all(blocks, AXES, split_axis=0, concat_axis=0, tiled=True)


def exchange_rows(rows, devices):
    wide = rows.reshape(devices, rows.shape[0] // devices, HALF)
    return pltpu.with_memory_space_constraint(exchange(wide).reshape(rows.shape), pltpu.VMEM)


def local(x, y, x_logmass, y_logmass, x_sizes, y_sizes, cross, xself, yself):
    devices = lax.axis_size(AXES)
    tables = (cross, xself.T, yself.T)
    send, weight, half, start_g, start = push(
        *tables, x_sizes, y_sizes, x, y,
        x_logmass.reshape(SPAN, HALF), y_logmass.reshape(SPAN, HALF), devices,
    )
    moved = exchange(send)
    left, right = left_side(x, y)
    left2, cols_local, log_own = local_tiles(left, right, start_g, start)
    back, cols_moved, index, listed = first_tiles(moved, left, left2, start_g, start)
    inbox = exchange_rows(back, devices)
    potential_g, bias_g = update_g(cols_local, cols_moved, weight, half, start_g)
    potential, bias, outbox = step(
        False, True, tables, index, moved,
        inbox, cols_local, log_own, cols_moved, weight, half, start_g, start, bias_g, left,
    )
    for iteration in range(1, ITERS):
        last = iteration == ITERS - 1
        inbox = exchange_rows(outbox, devices)
        _, cols_local, log_own = local_tiles(left, right, bias_g, bias)
        out = step(
            True, not last, tables, index, moved,
            inbox, cols_local, log_own, listed, weight, half, start_g, start,
            bias_g, bias, potential_g, potential, left, left2,
        )
        if not last:
            potential_g, bias_g, potential, bias, outbox = out
    return tuple(part.reshape(SPAN * HALF) for part in out)


def solution(mesh):
    flat, table = P(AXES), P(AXES, None)
    points = P(None, AXES)
    return jax.shard_map(
        local,
        mesh=mesh,
        in_specs=(points, points, flat, flat, table, table, table, table, table),
        out_specs=(flat, flat, flat, flat),
        check_vma=False,
    )
```

```python
import functools

import jax
import jax.numpy as jnp
from jax import lax
from jax.experimental import pallas as pl
from jax.experimental.pallas import tpu as pltpu
from jax.sharding import PartitionSpec as P

ITERS = 3
EPSILON = 0.5
DAMPING = 2.0 / (2.0 + 0.5)
NEGATIVE = -1e30
REAL = -1e29
LOG2E = 1.4426950408889634
LN2 = 0.6931471805599453
TINY = 2.0**-90
HUGE = 2.0**90
AXES = ("row", "col")

D = 64
CS = 256
CL = 8
HALF = 128
ROWS = 2 * D + 8
GROUP = 8
LOCAL_GROUP = 4
PIECES = 8
SPAN = 16
BF16 = jnp.bfloat16
F32 = jnp.float32


def lists(cross, xself, yself):
    for c in range(cross.shape[0]):
        for k in range(cross.shape[1]):
            yield 0, c, k, cross[c, k]
    for table, kind in ((xself, 1), (yself, 2)):
        for c in range(table.shape[1]):
            for k in range(table.shape[0]):
                yield kind, c, k, table[k, c]


def bias_of(weight, half, potential):
    return LOG2E * (weight + (potential - half) / EPSILON)


def push_kernel(
    cross, xself, yself, x_sizes, y_sizes, x_ref, y_ref, x_mass, y_mass,
    send, weight_ref, half_ref, bias_g_ref, bias_ref, aux, sems,
):
    devices = send.shape[0]
    requests = list(lists(cross, xself, yself))
    for kind, c, _, named in requests:
        owner = named // CL
        source = y_ref if kind == 2 else x_ref
        for h in range(2):
            pltpu.make_async_copy(
                source.at[:, pl.ds(c * CS + h * HALF, HALF)],
                send.at[owner, pl.ds(h * D, D), :],
                sems.at[0],
            ).start()
    row = lax.broadcasted_iota(jnp.int32, (2 * CL, HALF), 0)
    position = (row % 2) * HALF + lax.broadcasted_iota(jnp.int32, (2 * CL, HALF), 1)
    for side, (points, sizes, mass) in enumerate(
        ((x_ref, x_sizes, x_mass), (y_ref, y_sizes, y_mass))
    ):
        count = jnp.zeros((2 * CL, HALF), jnp.int32)
        for c in range(CL):
            count = jnp.where(row // 2 == c, sizes[0, c], count)
        base = side * 2 * CL
        weight_ref[base : base + 2 * CL, :] = jnp.where(position < count, mass[...], NEGATIVE)
        for t in range(2 * CL):
            piece = points[:, t * HALF : (t + 1) * HALF]
            half_ref[base + t : base + t + 1, :] = 0.5 * jnp.sum(piece * piece, axis=0, keepdims=True)
    bias = bias_of(weight_ref[...], half_ref[...], 0.0)
    bias_ref[0 : 2 * CL, :] = bias[0 : 2 * CL, :]
    bias_ref[2 * CL : 6 * CL, :] = bias
    bias_g_ref[...] = bias[2 * CL : 4 * CL, :]
    aux[...] = jnp.zeros_like(aux)
    for kind, c, _, named in requests:
        owner = named // CL
        base = kind * 2 * CL + 2 * c
        aux[owner, 0:2, :] = bias_ref[base : base + 2, :]
        code = (kind * CL + named % CL + 1).astype(F32)
        aux[owner, 2:3, :] = jnp.full((1, HALF), code, F32)
    tail = pltpu.make_async_copy(aux, send.at[:, pl.ds(2 * D, 8), :], sems.at[1])
    tail.start()
    tail.wait()
    sent = send.at[pl.ds(0, len(requests)), pl.ds(0, 2 * D), :]
    pltpu.make_async_copy(sent, sent, sems.at[0]).wait()


def push(cross, xself, yself, x_sizes, y_sizes, x, y, x_mass, y_mass, devices):
    smem = pl.BlockSpec(memory_space=pltpu.SMEM)
    vmem = pl.BlockSpec(memory_space=pltpu.VMEM)
    return pl.pallas_call(
        push_kernel,
        out_shape=(
            jax.ShapeDtypeStruct((devices, ROWS, HALF), F32),
            jax.ShapeDtypeStruct((4 * CL, HALF), F32),
            jax.ShapeDtypeStruct((4 * CL, HALF), F32),
            jax.ShapeDtypeStruct((2 * CL, HALF), F32),
            jax.ShapeDtypeStruct((6 * CL, HALF), F32),
        ),
        in_specs=[smem] * 5 + [vmem] * 4,
        out_specs=(pl.BlockSpec(memory_space=pl.ANY), vmem, vmem, vmem, vmem),
        scratch_shapes=[
            pltpu.VMEM((devices, 8, HALF), F32),
            pltpu.SemaphoreType.DMA((2,)),
        ],
        name="push",
    )(cross, xself, yself, x_sizes, y_sizes, x, y, x_mass, y_mass)


def split2(value):
    high = value.astype(BF16)
    return high, (value - high.astype(F32)).astype(BF16)


def split3(value):
    high = value.astype(BF16).astype(F32)
    rest = value - high
    middle = rest.astype(BF16).astype(F32)
    return high, middle, rest - middle


def left_kernel(x_ref, y_ref, left_ref, right_ref):
    lane = lax.broadcasted_iota(jnp.int32, (CS, HALF), 1)
    for side, points in enumerate((x_ref, y_ref)):
        for c in range(CL):
            piece = points[:, c * CS : (c + 1) * CS]
            scaled = piece * (LOG2E / EPSILON)
            turned = jnp.transpose(jnp.concatenate([scaled, scaled], axis=0))
            high, low = split2(turned)
            left_ref[side * CL + c, :, 0:HALF] = high
            low = jnp.where(lane < D, low.astype(F32), 0.0)
            left_ref[side * CL + c, :, HALF:CS] = low.astype(BF16)
            high, low = split2(piece)
            right_ref[side * CL + c, 0:D, :] = high
            right_ref[side * CL + c, D:HALF, :] = low


def left_side(x, y):
    vmem = pl.BlockSpec(memory_space=pltpu.VMEM)
    return pl.pallas_call(
        left_kernel,
        out_shape=(
            jax.ShapeDtypeStruct((2 * CL, CS, CS), BF16),
            jax.ShapeDtypeStruct((2 * CL, HALF, CS), BF16),
        ),
        in_specs=[vmem, vmem],
        out_specs=(vmem, vmem),
        name="left_side",
    )(x, y)


def scores(left_high, left_rest, high, low, a, e):
    a1, a2, a3 = split3(a)
    row = lax.broadcasted_iota(jnp.int32, (8, CS), 0)
    pick = jnp.where(row == e, 1.0, 0.0)
    mine = jnp.where(row == 0, a1, jnp.where(row == 1, a2, jnp.where(row == 2, a3, 0.0)))
    tail = jnp.concatenate([pick, pick, pick, mine], axis=0).astype(BF16)
    right = jnp.concatenate([high, low, high, tail, jnp.zeros((32, CS), BF16)], axis=0)
    return jnp.dot(
        jnp.concatenate([left_high, left_rest], axis=1), right, preferred_element_type=F32
    )


def put_row(out, at, value):
    out[pl.ds(at, 1), :] = value[:, 0:HALF]
    out[pl.ds(at + 1, 1), :] = value[:, HALF:CS]


def row_sum(value, a):
    return jnp.where(a > REAL, jnp.sum(value, axis=0, keepdims=True), 1.0)


def fold(value):
    return value[:, 0:HALF] + value[:, HALF:CS]


def row_log_sum(z):
    peak = jnp.max(z, axis=0, keepdims=True)
    total = jnp.sum(jnp.exp2(z - peak), axis=0, keepdims=True)
    return peak + jnp.log(total) * LOG2E


def merge_columns(z, te, acc, top):
    peak = jnp.max(z, axis=1, keepdims=True)
    total = jnp.sum(jnp.exp2(z - peak), axis=1, keepdims=True)
    before = top[te]
    now = jnp.maximum(before, peak)
    acc[te] = acc[te] * jnp.exp2(before - now) + total * jnp.exp2(peak - now)
    top[te] = now


def columns(acc, top, cols):
    lane = lax.broadcasted_iota(jnp.int32, (CS, HALF), 1)
    batch = 1 if top is not None else 8

    def some(i, packed):
        for j in range(batch):
            te = i * batch + j
            if top is not None:
                value = jnp.max(top[te] + jnp.log(acc[te]) * LOG2E, axis=1, keepdims=True)
            else:
                value = jnp.sum(acc[te], axis=1, keepdims=True)
            packed = jnp.where(lane == te, value, packed)
        return packed

    packed = lax.fori_loop(0, 3 * CL // batch, some, jnp.zeros((CS, HALF), F32))
    for h in range(2):
        turned = jnp.transpose(packed[h * HALF : (h + 1) * HALF, :])
        for t in range(3):
            cols[pl.ds(t * 2 * CL + h, CL, stride=2), :] = turned[t * CL : (t + 1) * CL, :]


def in_range(*values):
    lowest = functools.reduce(jnp.minimum, [jnp.min(value) for value in values])
    highest = functools.reduce(jnp.maximum, [jnp.max(value) for value in values])
    return jnp.logical_and(lowest > TINY, highest < HUGE)


def build_left2(left, bias_g, bias, left2, kinds=(0, 1, 2)):
    row8 = lax.broadcasted_iota(jnp.int32, (8, HALF), 0)
    ones = jnp.where(row8 < 3, 1.0, 0.0)
    for t in kinds:
        for h in range(2):
            if t == 0:
                value = bias_g[pl.ds(h, CL, stride=2), :]
            else:
                value = bias[pl.ds(t * SPAN + h, CL, stride=2), :]
            high, middle, low = split3(value)
            stack = jnp.concatenate(
                [jnp.zeros((D, HALF), F32), high, middle, low, ones, jnp.zeros((32, HALF), F32)], axis=0
            )
            turned = jnp.transpose(stack).astype(BF16)
            for e in range(CL):
                cluster = e if t == 1 else CL + e
                here = pl.ds(h * HALF, HALF)
                left2[t * CL + e, here, :] = left[cluster, here, pl.ds(HALF, HALF)] + turned


def local_kernel(left, right, bias_g, bias, left2, log_cols, log_own, acc, top, own):
    span = SPAN
    build_left2(left, bias_g, bias, left2)

    def sweep(finish):
        for t in range(3):

            def some(i, _):
                for j in range(LOCAL_GROUP):
                    e = i * LOCAL_GROUP + j
                    at = t * span + 2 * e
                    a = jnp.concatenate([bias[pl.ds(at, 1), :], bias[pl.ds(at + 1, 1), :]], axis=1)
                    source = CL + e if t == 2 else e
                    z = scores(
                        left[e if t == 1 else CL + e, :, 0:HALF], left2[t * CL + e],
                        right[source, 0:D, :], right[source, D:HALF, :], a, e,
                    )
                    finish(z, a, t, e)
                return 0

            lax.fori_loop(0, CL // LOCAL_GROUP, some, 0)

    def fast(z, a, t, e):
        value = jnp.exp2(z)
        if t == 0:
            put_row(own, 2 * e, row_sum(value, a))
        acc[t * CL + e] = fold(value)

    def slow(z, a, t, e):
        if t == 0:
            put_row(own, 2 * e, row_log_sum(z))
        merge_columns(z, t * CL + e, acc, top)

    sweep(fast)
    columns(acc, None, log_cols)
    real = jnp.concatenate([bias_g[...], bias[span : 3 * span, :]], axis=0) > REAL
    cols = jnp.where(real, log_cols[...], 1.0)
    within = in_range(own[...], cols)

    @pl.when(within)
    def _():
        log_own[...] = jnp.log(own[...]) * LOG2E
        log_cols[...] = jnp.log(cols) * LOG2E

    @pl.when(jnp.logical_not(within))
    def _():
        acc[...] = jnp.zeros_like(acc)
        top[...] = jnp.full_like(top, 3.0 * NEGATIVE)
        sweep(slow)
        columns(acc, top, log_cols)
        log_own[...] = own[...]


def local_tiles(left, right, bias_g, bias):
    vmem = pl.BlockSpec(memory_space=pltpu.VMEM)
    return pl.pallas_call(
        local_kernel,
        out_shape=(
            jax.ShapeDtypeStruct((3 * CL, CS, HALF), BF16),
            jax.ShapeDtypeStruct((6 * CL, HALF), F32),
            jax.ShapeDtypeStruct((2 * CL, HALF), F32),
        ),
        in_specs=[vmem] * 4,
        out_specs=(vmem,) * 3,
        scratch_shapes=[
            pltpu.VMEM((3 * CL, CS, HALF), F32),
            pltpu.VMEM((3 * CL, CS, HALF), F32),
            pltpu.VMEM((2 * CL, HALF), F32),
        ],
        name="local_tiles",
    )(left, right, bias_g, bias)


def fetch_all(moved, held, sems):
    step = moved.shape[0] // PIECES

    def fetch(i):
        part = pl.ds(i * step, step)
        return pltpu.make_async_copy(moved.at[part], held.at[part], sems.at[i])

    for i in range(PIECES):
        fetch(i).start()
    return fetch


def bring(pairs, sems, base):
    copies = [pltpu.make_async_copy(a, b, sems.at[base + i]) for i, (a, b) in enumerate(pairs)]
    for copy in copies:
        copy.start()
    return copies


class Tiles:
    def __init__(self, held, left, slots, targets, live, bounds=None):
        self.held, self.left = held, left
        self.slots, self.targets, self.live, self.bounds = slots, targets, live, bounds
        self.devices = held.shape[0]

    def run(self, size, left2, inbox, finish):
        held, left = self.held, self.left

        def body(i, _):
            for j in range(size):
                n = i * size + j
                s, te = self.slots[n], self.targets[n]
                e = te % CL
                cluster = jnp.where(te // CL == 1, e, CL + e)
                spot = jnp.where(n < self.live, s, self.devices)
                high, low = split2(jnp.concatenate([held[s, 0:D, :], held[s, D : 2 * D, :]], axis=1))
                if inbox is None:
                    pair = held[s, 2 * D : 2 * D + 1, :], held[s, 2 * D + 1 : 2 * D + 2, :]
                else:
                    pair = inbox[pl.ds(4 * s + 2, 1), :], inbox[pl.ds(4 * s + 3, 1), :]
                a = jnp.where(n < self.live, jnp.concatenate(pair, axis=1), LOG2E * NEGATIVE)
                z = scores(left[cluster, :, 0:HALF], left2[te], high, low, a, e)
                finish(z, a, te, spot)
            return 0

        return body

    def sweep(self, left2, inbox, finish, fetch=None):
        run = self.run(GROUP, left2, inbox, finish)
        groups = (self.live + GROUP - 1) // GROUP
        if fetch is None:
            lax.fori_loop(0, groups, run, 0)
            return
        step = self.devices // PIECES

        def piece(i, start):
            fetch(i).wait()
            ready = self.bounds[(i + 1) * step - 1]
            stop = jnp.where(i == PIECES - 1, groups, ready // GROUP)
            lax.fori_loop(start, stop, run, 0)
            return stop

        lax.fori_loop(0, PIECES, piece, 0)

    def slow_sweep(self, left2, inbox, finish):
        lax.fori_loop(0, self.live, self.run(1, left2, inbox, finish), 0)


def column_pass(tiles, left2, inbox, fetch, acc, top, cols, start_g, start, named, sums=None):
    def fast(z, a, te, spot):
        value = jnp.exp2(z)
        if sums is not None:
            put_row(sums, 2 * spot, row_sum(value, a))
        acc[te] = acc[te] + fold(value)

    def slow(z, a, te, spot):
        if sums is not None:
            put_row(sums, 2 * spot, row_log_sum(z))
        merge_columns(z, te, acc, top)

    tiles.sweep(left2, inbox, fast, fetch)
    columns(acc, None, cols)
    real = jnp.concatenate([start_g[...], start[SPAN : 3 * SPAN, :]], axis=0) > REAL
    linear = jnp.where(jnp.logical_and(real, named), cols[...], 1.0)
    within = in_range(linear) if sums is None else in_range(sums[...], linear)

    @pl.when(within)
    def _():
        cols[...] = jnp.where(named, jnp.log(linear) * LOG2E, NEGATIVE)

    @pl.when(jnp.logical_not(within))
    def _():
        acc[...] = jnp.zeros_like(acc)
        top[...] = jnp.full_like(top, 3.0 * NEGATIVE)
        tiles.slow_sweep(left2, inbox, slow)
        columns(acc, top, cols)
        cols[...] = jnp.where(named, cols[...], NEGATIVE)

    return within


def row_pass(tiles, left2, sums, fetch=None):
    def fast(z, a, te, spot):
        put_row(sums, 4 * spot, row_sum(jnp.exp2(z), a))

    def slow(z, a, te, spot):
        put_row(sums, 4 * spot, row_log_sum(z))

    tiles.sweep(left2, None, fast, fetch)
    within = in_range(sums[...])

    @pl.when(within)
    def _():
        sums[...] = jnp.log(sums[...]) * LOG2E

    @pl.when(jnp.logical_not(within))
    def _():
        sums[...] = jnp.zeros_like(sums)
        tiles.slow_sweep(left2, None, slow)


def first_kernel(
    moved, left_hbm, left2_hbm, start_g, start, back, log_cols, slots, targets, bounds, listed,
    held, acc, top, sums, codes, count, sems, left, left2,
):
    devices = moved.shape[0]
    tags = pltpu.make_async_copy(moved.at[:, pl.ds(2 * D + 2, 1), :], codes, sems.at[PIECES])
    tags.start()
    sides = bring(((left_hbm, left), (left2_hbm, left2)), sems, PIECES + 1)
    fetch = fetch_all(moved, held, sems)
    acc[...] = jnp.zeros_like(acc)
    sums[...] = jnp.ones_like(sums)
    for te in range(3 * CL):
        count[te] = 0
    tags.wait()

    def gather(s, n):
        code = codes[s, 0, 0].astype(jnp.int32)

        @pl.when(code > 0)
        def _():
            slots[n] = s
            targets[n] = code - 1
            count[code - 1] = 1

        n = n + (code > 0).astype(jnp.int32)
        bounds[s] = n
        return n

    live = lax.fori_loop(0, devices, gather, 0, unroll=8)
    row = lax.broadcasted_iota(jnp.int32, listed.shape, 0) // 2
    some_listed = jnp.zeros(listed.shape, jnp.int32)
    for te in range(3 * CL):
        some_listed = jnp.where(row == te, count[te], some_listed)
    listed[...] = some_listed
    for i in range(GROUP):
        slots[live + i] = slots[0]
        targets[live + i] = 0
    tiles = Tiles(held, left, slots, targets, live, bounds)
    named = some_listed > 0
    for copy in sides:
        copy.wait()
    within = column_pass(tiles, left2, None, fetch, acc, top, log_cols, start_g, start, named, sums)

    @pl.when(within)
    def _():
        back[...] = jnp.log(sums[0 : 2 * devices, :]) * LOG2E

    @pl.when(jnp.logical_not(within))
    def _():
        back[...] = sums[0 : 2 * devices, :]


SMEM = pl.BlockSpec(memory_space=pltpu.SMEM)
VMEM = pl.BlockSpec(memory_space=pltpu.VMEM)
HBM = pl.BlockSpec(memory_space=pl.ANY)


def shape(*dims, dtype=F32):
    return jax.ShapeDtypeStruct(dims, dtype)


def first_tiles(moved, left, left2, start_g, start):
    devices = moved.shape[0]
    out = pl.pallas_call(
        first_kernel,
        out_shape=(
            shape(2 * devices, HALF),
            shape(3 * SPAN, HALF),
            shape(devices + GROUP, dtype=jnp.int32),
            shape(devices + GROUP, dtype=jnp.int32),
            shape(devices, dtype=jnp.int32),
            shape(3 * SPAN, HALF, dtype=jnp.int32),
        ),
        in_specs=[HBM] * 3 + [VMEM] * 2,
        out_specs=(VMEM, VMEM, SMEM, SMEM, SMEM, VMEM),
        scratch_shapes=[
            pltpu.VMEM((devices, ROWS, HALF), F32),
            pltpu.VMEM((3 * CL, CS, HALF), F32),
            pltpu.VMEM((3 * CL, CS, HALF), F32),
            pltpu.VMEM((2 * devices + 8, HALF), F32),
            pltpu.SMEM((devices, 1, HALF), F32),
            pltpu.SMEM((3 * CL,), jnp.int32),
            pltpu.SemaphoreType.DMA((PIECES + 3,)),
            pltpu.VMEM((2 * CL, CS, CS), BF16),
            pltpu.VMEM((3 * CL, CS, HALF), BF16),
        ],
        name="first_tiles",
    )(moved, left, left2, start_g, start)
    return out[0], out[1], out[2:5], out[5]


def log_sum(values):
    peak = functools.reduce(jnp.maximum, values)
    total = functools.reduce(jnp.add, [jnp.exp2(value - peak) for value in values])
    return peak + jnp.log(total) * LOG2E


def fresh(total, weight, half, potential):
    value = 0.5 * (potential - DAMPING * EPSILON * (LN2 * total - half / EPSILON))
    return jnp.where(weight > REAL, value, 0.0)


def cross_kernel(
    slots, targets, bounds, moved, left_hbm, cols_local, cols_moved, weight, half, start_g,
    new, new_bias, partial, self_slots, self_targets, self_bounds,
    held, left, left2, sums, cross_slots, cross_targets, sems,
):
    devices = moved.shape[0]
    sides = bring(((left_hbm, left),), sems, PIECES)
    fetch = fetch_all(moved, held, sems)
    side, span = slice(SPAN, 2 * SPAN), slice(0, SPAN)
    total = log_sum([cols_local[span, :], cols_moved[span, :]]) - start_g[...]
    value = fresh(total, weight[side, :], half[side, :], 0.0)
    new[...] = value
    new_bias[...] = bias_of(weight[side, :], half[side, :], value)

    def sort(n, found):
        s, te = slots[n], targets[n]
        mine = te < CL

        @pl.when(mine)
        def _():
            cross_slots[found] = s
            cross_targets[found] = te

        @pl.when(jnp.logical_not(mine))
        def _():
            self_slots[n - found] = s
            self_targets[n - found] = te

        return found + mine.astype(jnp.int32)

    live = bounds[devices - 1]
    found = lax.fori_loop(0, live, sort, 0)
    self_bounds[devices - 1] = live - found
    for i in range(GROUP):
        cross_slots[found + i] = cross_slots[0]
        cross_targets[found + i] = 0
        self_slots[live - found + i] = self_slots[0]
        self_targets[live - found + i] = 0
    sums[...] = jnp.ones_like(sums)
    for copy in sides:
        copy.wait()
    build_left2(left, new_bias, None, left2, (0,))
    for i in range(PIECES):
        fetch(i).wait()
    row_pass(Tiles(held, left, cross_slots, cross_targets, found), left2, sums)
    partial[...] = sums[0 : 4 * devices, :]


def cross_rows(index, moved, left, *args):
    devices = moved.shape[0]
    many = devices + GROUP
    out = pl.pallas_call(
        cross_kernel,
        out_shape=(
            shape(SPAN, HALF),
            shape(SPAN, HALF),
            shape(4 * devices, HALF),
            shape(many, dtype=jnp.int32),
            shape(many, dtype=jnp.int32),
            shape(devices, dtype=jnp.int32),
        ),
        in_specs=[SMEM] * 3 + [HBM] * 2 + [VMEM] * 5,
        out_specs=(VMEM,) * 3 + (SMEM,) * 3,
        scratch_shapes=[
            pltpu.VMEM((devices, ROWS, HALF), F32),
            pltpu.VMEM((2 * CL, CS, CS), BF16),
            pltpu.VMEM((CL, CS, HALF), BF16),
            pltpu.VMEM((4 * devices + 8, HALF), F32),
            pltpu.SMEM((many,), jnp.int32),
            pltpu.SMEM((many,), jnp.int32),
            pltpu.SemaphoreType.DMA((PIECES + 1,)),
        ],
        name="cross_rows",
    )(*index, moved, left, *args)
    return out[0], out[1], out[2], out[3:]


def step_kernel(has_columns, has_rows, *refs):
    refs = list(refs)
    take = lambda n: [refs.pop(0) for _ in range(n)]
    cross, xself, yself, slots, targets, bounds, moved = take(7)
    inbox, cols_local, log_own, cols_moved, weight, half, start_g, start = take(8)
    if has_columns:
        listed = cols_moved
        bias_g, bias, potential_g, potential, left_hbm, left2_hbm = take(6)
    else:
        bias = start
        new_bias_g, partial, left_hbm = take(3)
    if not has_rows:
        new_f, new_g, new_p, new_q = take(4)
    else:
        new_g, new_bias_g = take(2) if has_columns else (None, new_bias_g)
        new, new_bias, outbox = take(3)
    held, parts, sems, left = take(4)
    if has_columns:
        acc, top, cols_moved, left2_start = take(4)
    if has_rows:
        left2, sums = take(2)
    devices = moved.shape[0]
    pairs = ((left_hbm, left), (left2_hbm, left2_start)) if has_columns else ((left_hbm, left),)
    sides = bring(pairs, sems, PIECES)
    fetch = fetch_all(moved, held, sems)
    counts = (cross.shape[1], xself.shape[0], yself.shape[0])
    offsets = (0, counts[0], counts[0] + counts[1])
    requests = list(lists(cross, xself, yself))
    width = inbox.shape[0] // devices
    for kind, c, k, wanted in requests:
        at = pl.multiple_of(width * (wanted // CL), width)
        parts[offsets[kind] + k, 2 * c : 2 * c + 2, :] = inbox[pl.ds(at, 2), :]
    if has_rows:
        sums[...] = jnp.ones_like(sums)
    tiles = Tiles(held, left, slots, targets, bounds[devices - 1], bounds)
    if has_columns:
        acc[...] = jnp.zeros_like(acc)
    for copy in sides:
        copy.wait()
    if not has_columns:
        for i in range(PIECES):
            fetch(i).wait()
    if has_columns:
        column_pass(
            tiles, left2_start, inbox, fetch, acc, top, cols_moved, start_g, start, listed[...] > 0
        )
    f, p, q = (slice(i * SPAN, (i + 1) * SPAN) for i in range(3))
    answers = [
        [parts[offsets[t] + k] - start[t * SPAN : (t + 1) * SPAN, :] for k in range(counts[t])]
        for t in range(3)
    ]
    totals = [log_sum([log_own[...] - bias[f, :]] + answers[0])]
    for here, answer in ((p, answers[1]), (q, answers[2])):
        totals.append(
            log_sum([cols_local[here, :] - bias[here, :], cols_moved[here, :] - start[here, :]] + answer)
        )
    for i, total in enumerate(totals):
        here = (f, p, q)[i]
        side = slice(SPAN, 2 * SPAN) if i == 2 else slice(0, SPAN)
        before = potential[here, :] if has_columns else 0.0
        value = fresh(total, weight[side, :], half[side, :], before)
        if has_rows:
            new[here, :] = value
            new_bias[here, :] = bias_of(weight[side, :], half[side, :], value)
        else:
            (new_f, new_p, new_q)[i][...] = value
    if has_columns:
        side = slice(SPAN, 2 * SPAN)
        total = log_sum([cols_local[f, :] - bias_g[...], cols_moved[f, :] - start_g[...]])
        value = fresh(total, weight[side, :], half[side, :], potential_g[...])
        new_g[...] = value
        if has_rows:
            new_bias_g[...] = bias_of(weight[side, :], half[side, :], value)
    if not has_rows:
        return
    for kind, c, _, wanted in requests:
        at = pl.multiple_of(4 * (wanted // CL) + 2, 2)
        base = kind * SPAN + 2 * c
        outbox[pl.ds(at, 2), :] = new_bias[base : base + 2, :]
    build_left2(left, new_bias_g, new_bias, left2, (0, 1, 2) if has_columns else (1, 2))

    row_pass(tiles, left2, sums)
    answer = sums[0 : 4 * devices, :]
    if not has_columns:
        answer = answer + partial[...]
    answer_row = lax.broadcasted_iota(jnp.int32, outbox.shape, 0) % 4 < 2
    outbox[...] = jnp.where(answer_row, answer, outbox[...])


def step(has_columns, has_rows, tables, index, moved, *args):
    devices = moved.shape[0]
    listed = tables[0].shape[1] + tables[1].shape[0] + tables[2].shape[0]
    one, three = shape(SPAN, HALF), shape(3 * SPAN, HALF)
    sides = 2 if has_columns else 1
    if has_rows:
        outs = ([one, one] if has_columns else []) + [three, three, shape(4 * devices, HALF)]
    else:
        outs = [one] * 4
    scratch = [
        pltpu.VMEM((devices, ROWS, HALF), F32),
        pltpu.VMEM((listed, SPAN, HALF), F32),
        pltpu.SemaphoreType.DMA((PIECES + 2,)),
        pltpu.VMEM((2 * CL, CS, CS), BF16),
    ]
    if has_columns:
        scratch += [pltpu.VMEM((3 * CL, CS, HALF), F32)] * 2
        scratch += [pltpu.VMEM((3 * SPAN, HALF), F32), pltpu.VMEM((3 * CL, CS, HALF), BF16)]
    if has_rows:
        scratch += [pltpu.VMEM((3 * CL, CS, HALF), BF16), pltpu.VMEM((4 * devices + 8, HALF), F32)]
    return pl.pallas_call(
        functools.partial(step_kernel, has_columns, has_rows),
        out_shape=outs,
        in_specs=[SMEM] * 6 + [HBM] + [VMEM] * (len(args) - sides) + [HBM] * sides,
        out_specs=[VMEM] * len(outs),
        scratch_shapes=scratch,
        name="step_" + "c" * has_columns + "r" * has_rows,
    )(*tables, *index, moved, *args)


def exchange(blocks):
    return lax.all_to_all(blocks, AXES, split_axis=0, concat_axis=0, tiled=True)


def exchange_rows(rows, devices):
    wide = rows.reshape(devices, rows.shape[0] // devices, HALF)
    return pltpu.with_memory_space_constraint(exchange(wide).reshape(rows.shape), pltpu.VMEM)


def local(x, y, x_logmass, y_logmass, x_sizes, y_sizes, cross, xself, yself):
    devices = lax.axis_size(AXES)
    tables = (cross, xself.T, yself.T)
    send, weight, half, start_g, start = push(
        *tables, x_sizes, y_sizes, x, y,
        x_logmass.reshape(SPAN, HALF), y_logmass.reshape(SPAN, HALF), devices,
    )
    moved = exchange(send)
    left, right = left_side(x, y)
    left2, cols_local, log_own = local_tiles(left, right, start_g, start)
    back, cols_moved, index, listed = first_tiles(moved, left, left2, start_g, start)
    inbox = exchange_rows(back, devices)
    potential_g, bias_g, partial, self_index = cross_rows(
        index, moved, left, cols_local, cols_moved, weight, half, start_g
    )
    potential, bias, outbox = step(
        False, True, tables, self_index, moved,
        inbox, cols_local, log_own, cols_moved, weight, half, start_g, start, bias_g, partial, left,
    )
    for iteration in range(1, ITERS):
        last = iteration == ITERS - 1
        inbox = exchange_rows(outbox, devices)
        _, cols_local, log_own = local_tiles(left, right, bias_g, bias)
        out = step(
            True, not last, tables, index, moved,
            inbox, cols_local, log_own, listed, weight, half, start_g, start,
            bias_g, bias, potential_g, potential, left, left2,
        )
        if not last:
            potential_g, bias_g, potential, bias, outbox = out
    return tuple(part.reshape(SPAN * HALF) for part in out)


def solution(mesh):
    flat, table = P(AXES), P(AXES, None)
    points = P(None, AXES)
    return jax.shard_map(
        local,
        mesh=mesh,
        in_specs=(points, points, flat, flat, table, table, table, table, table),
        out_specs=(flat, flat, flat, flat),
        check_vma=False,
    )
```
